128 devices in a mesh: gy: 8 (over x, core), gx: 16 (over z, y).
Axes of the slice: x: 4, y: 4, z: 4, core: 2. Of those that a mesh axis runs over, the one named last changes fastest.
Arguments:
- model_field: float32 [60, 2048, 2048], P(None, 'gy', 'gx'), may hold values from -160 to 160
- driver_field: float32 [60, 2048, 2048], P(None, 'gy', 'gx'), may hold values from -60 to 60
- nudge_rate: float32 [60], replicated, may hold values from 0.1 to 0.5
- increment_cap: float32 [60], replicated, may hold values from 1 to 3
Outputs:
- nudged: float32 [60, 2048, 2048], P(None, 'gy', 'gx')
The draws below stay inside these ranges and needn't reach their ends.
All inputs are finite; a program needn't handle non-finite values.
Results may differ from the reference program's by a relative error of at most 0.00005.
Values sent between devices are 32-bit elements; how exact they have to be, the bound alone decides.
No kernel may reach another device: no remote copies, remote signals or barrier semaphores. Data moves between devices by JAX's collectives and lax.ppermute only.
A program may use at most 64 MiB of HBM per device.

```python
import math
import jax
import jax.numpy as jnp
from jax import lax

MODES = 24
FIELDS = 60
NY = 2048
NX = 2048


def driver_table(length_all):
    positions = lax.iota(jnp.int32, length_all)
    wavenumber = jnp.concatenate([lax.iota(jnp.int32, 32), lax.iota(jnp.int32, 32) + 1])
    phases = positions[:, None] * wavenumber[None, :] % length_all
    angles = phases.astype(jnp.float32) * (2.0 * math.pi / length_all)
    column = lax.iota(jnp.int32, 64)
    return jnp.where(column[None, :] < 32, jnp.cos(angles), jnp.sin(angles))


def field_amplitude(key):
    order_key, offset_key = jax.random.split(jax.random.fold_in(key, 97), 2)
    order = jax.random.permutation(order_key, FIELDS).astype(jnp.float32)
    offset = jax.random.uniform(offset_key, (FIELDS,), jnp.float32, 0.0, 1.0)
    logs = math.log(0.05) + (order + offset) / FIELDS * math.log(40.0)
    return jnp.exp(logs)


def draw_model_field(key, part):
    first, second, third = jax.random.split(jax.random.fold_in(key, 11), 3)
    amplitude = field_amplitude(key)[:, None, None]
    growth = 0.5 * math.log(3.0)
    noise = jnp.clip(jax.random.normal(first, (FIELDS, NY, NX), jnp.float32), -5.0, 5.0)
    trend_rows = jnp.exp(growth * lax.iota(jnp.int32, NY).astype(jnp.float32) / NY)
    trend_columns = jnp.exp(growth * lax.iota(jnp.int32, NX).astype(jnp.float32) / NX)
    scale_rows = jnp.exp(jax.random.uniform(second, (NY,), jnp.float32, 0.0, 0.5 * math.log(10.0)))
    scale_columns = jnp.exp(jax.random.uniform(third, (NX,), jnp.float32, 0.0, 0.5 * math.log(10.0)))
    rows_factor = (trend_rows * scale_rows)[None, :, None]
    columns_factor = (trend_columns * scale_columns)[None, None, :]
    return 0.5 * noise * rows_factor * columns_factor * amplitude


def draw_driver_field(key, part):
    first, second = jax.random.split(jax.random.fold_in(key, 23), 2)
    amplitude = field_amplitude(key)[:, None, None]
    highest = lax.Precision.HIGHEST
    weights = jax.random.normal(first, (FIELDS, 64, 64), jnp.float32) * (3.0 / 32.0)
    table_rows = driver_table(NY)
    table_columns = driver_table(NX)
    rows_part = jnp.einsum('yj,fjk->fyk', table_rows, weights, precision=highest)
    smooth = jnp.einsum('fyk,xk->fyx', rows_part, table_columns, precision=highest)
    smooth = jnp.clip(smooth, -25.0, 25.0)
    rough = jnp.clip(jax.random.normal(second, (FIELDS, NY, NX), jnp.float32), -5.0, 5.0)
    return (smooth + 0.2 * rough) * amplitude


def setup_inputs(seed: int = 0) -> dict:
    keys = jax.random.split(jax.random.key(seed), 5)
    return {
        "model_field": draw_model_field(jax.random.fold_in(keys[4], 71), 0),
        "driver_field": draw_driver_field(jax.random.fold_in(keys[4], 71), 0),
        "nudge_rate": jnp.clip(jnp.exp(jax.random.uniform(keys[2], (FIELDS,), jnp.float32, math.log(0.1), math.log(0.5))), 0.1, 0.5),
        "increment_cap": jnp.clip(jnp.exp(jax.random.uniform(keys[3], (FIELDS,), jnp.float32, math.log(1.0), math.log(3.0))), 1.0, 3.0),
    }


epsilon = 1e-06

def basis_table(cell_count, start, length_all):
    positions = start + lax.iota(jnp.int32, cell_count)
    wavenumber = jnp.concatenate([lax.iota(jnp.int32, MODES), lax.iota(jnp.int32, MODES) + 1])
    phases = positions[:, None] * wavenumber[None, :] % length_all
    angles = phases.astype(jnp.float32) * (2.0 * math.pi / length_all)
    column = lax.iota(jnp.int32, 2 * MODES)
    weights = jnp.where(column == 0, math.sqrt(1.0 / length_all), math.sqrt(2.0 / length_all))
    return jnp.where(column[None, :] < MODES, jnp.cos(angles), jnp.sin(angles)) * weights[None, :]

def reference(model_field, driver_field, nudge_rate, increment_cap):
    highest = lax.Precision.HIGHEST
    basis_rows = basis_table(NY, 0, NY)
    basis_columns = basis_table(NX, 0, NX)

    def analyse(field_pair):
        model_slab, driver_slab = field_pair
        difference = driver_slab - model_slab
        along_x = jnp.dot(difference, basis_columns, precision=highest)
        coefficient = jnp.dot(basis_rows.T, along_x, precision=highest)
        return (jnp.sum(difference * difference), coefficient)
    squares, coefficients = lax.map(analyse, (model_field, driver_field))
    spread = jnp.sqrt(squares / (NY * NX) + epsilon)
    strength = nudge_rate * jnp.minimum(1.0, increment_cap / spread)

    def build(entries):
        model_slab, coefficient, strength_one = entries
        rows_part = jnp.dot(basis_rows, coefficient, precision=highest)
        large_scale = jnp.dot(rows_part, basis_columns.T, precision=highest)
        return model_slab + strength_one * large_scale
    return lax.map(build, (model_field, coefficients, strength))
```

```python
import numpy as np

import jax
import jax.numpy as jnp
import ml_dtypes
from jax import lax
from jax.experimental import pallas as pl
from jax.experimental.pallas import tpu as pltpu
from jax.sharding import Mesh
from jax.sharding import PartitionSpec as P

MODES = 24
WAVES = 2 * MODES
GROUP = 10
BLOCK = 5
TILES = 4
LANES = 128
SLOTS = 16
CHIP = ("x", "z", "y")
EPSILON = 1e-06


def basis_table(length):
    positions = np.arange(length)
    wavenumber = np.concatenate([np.arange(MODES), np.arange(MODES) + 1])
    phases = positions[:, None] * wavenumber[None, :] % length
    angles = phases * (2.0 * np.pi / length)
    column = np.arange(WAVES)
    weights = np.where(column == 0, np.sqrt(1.0 / length), np.sqrt(2.0 / length))
    return np.where(column[None, :] < MODES, np.cos(angles), np.sin(angles)) * weights[None, :]


def split_table(length, parts):
    table = basis_table(length).astype(np.float32)
    high = table.astype(ml_dtypes.bfloat16)
    low = (table - high.astype(np.float32)).astype(ml_dtypes.bfloat16)
    shape = (parts, length // parts, WAVES)
    return high.reshape(shape), low.reshape(shape)


def split(value):
    high = value.astype(jnp.bfloat16)
    low = (value - high.astype(jnp.float32)).astype(jnp.bfloat16)
    return high, low


def dot(left, right, contract):
    return lax.dot_general(left, right, (contract, ((), ())), preferred_element_type=jnp.float32)


def analysis_kernel(where, model, driver, rows, columns, mine, other, along_y, squares):
    step = pl.program_id(0)
    odd = step % 2

    @pl.when(step == 0)
    def _():
        along_y[...] = jnp.zeros_like(along_y)
        squares[...] = jnp.zeros_like(squares)

    for i in range(BLOCK):
        difference = driver[i] - model[i]
        field = odd * BLOCK + i
        squares[pl.ds(field, 1), :] = jnp.sum(difference * difference, axis=0, keepdims=True)
        parts = jnp.concatenate(split(difference), axis=1)
        product = dot(rows[0], parts, ((1,), (0,)))
        product = product[:WAVES] + product[WAVES:]
        high, low = split(product[:, :LANES] + product[:, LANES:])
        place = pl.ds(pl.multiple_of(field * WAVES, 16), WAVES)
        along_y[place, :LANES] = high
        along_y[place, LANES:] = low

    @pl.when(odd == 1)
    def _():
        both = dot(columns[0], along_y[...], ((1,), (1,)))
        both = both[:WAVES] + both[WAVES:]
        tiles = [both[:, t * LANES : (t + 1) * LANES] for t in range(TILES)]
        total = jnp.sum(squares[...], axis=1, keepdims=True)
        lane = lax.broadcasted_iota(jnp.int32, (SLOTS, LANES), 1)
        top = jnp.where(lane == LANES - 1, total, tiles[-1][:SLOTS])
        tiles[-1] = jnp.concatenate([top, tiles[-1][SLOTS:]], axis=0)
        group = step // 2
        half = group // 3
        first = pl.multiple_of((group % 3) * (TILES * WAVES), 8)

        def keep(ref):
            for t in range(TILES):
                ref[pl.ds(first + t * WAVES, WAVES), :] = tiles[t]

        pl.when(half == where[2])(lambda: keep(mine))
        pl.when(half != where[2])(lambda: keep(other))


def synthesis_kernel(
    cells, where, model, own, sibling, rate, cap, rows, columns, nudged, along_x, strength
):
    step = pl.program_id(0)
    odd = step % 2

    def prepare(ref):
        first = pl.multiple_of(((step // 2) % 3) * (TILES * WAVES), 8)
        tiles = [ref[pl.ds(first + t * WAVES, WAVES), :] for t in range(TILES)]
        total = tiles[-1][:SLOTS, LANES - 1 :]
        spread = jnp.sqrt(total / cells + EPSILON)
        strength[...] = rate[0] * jnp.minimum(1.0, cap[0] / spread)
        high, low = split(jnp.concatenate(tiles, axis=1))
        both = dot(high, columns[0], ((0,), (0,))) + dot(low, columns[0], ((0,), (0,)))
        along_x[...] = both[:, :LANES] + both[:, LANES:]

    pl.when((odd == 0) & (step < 6))(lambda: prepare(own))
    pl.when((odd == 0) & (step >= 6))(lambda: prepare(sibling))

    for i in range(BLOCK):
        field = odd * BLOCK + i
        place = pl.ds(pl.multiple_of(field * WAVES, 8), WAVES)
        high, low = split(along_x[place, :] * strength[pl.ds(field, 1), :])
        stack = jnp.concatenate([high, low, high], axis=0)
        nudged[i] = model[i] + dot(rows[0], stack, ((1,), (0,)))


def analysis(where, model, driver, rows, columns):
    fields, height, width = model.shape
    steps = fields // BLOCK
    half = fields // GROUP // 2 * TILES * WAVES
    block = pl.BlockSpec((BLOCK, height, width), lambda s, w: (s, 0, 0))
    whole = pl.BlockSpec((half, LANES), lambda s, w: (0, 0))
    return pl.pallas_call(
        analysis_kernel,
        out_shape=[jax.ShapeDtypeStruct((half, LANES), jnp.float32)] * 2,
        grid_spec=pltpu.PrefetchScalarGridSpec(
            num_scalar_prefetch=1,
            grid=(steps,),
            in_specs=[
                block,
                block,
                pl.BlockSpec((1, *rows.shape[1:]), lambda s, w: (w[0], 0, 0)),
                pl.BlockSpec((1, *columns.shape[1:]), lambda s, w: (w[1], 0, 0)),
            ],
            out_specs=[whole, whole],
            scratch_shapes=[
                pltpu.VMEM((TILES * LANES, 2 * LANES), jnp.bfloat16),
                pltpu.VMEM((SLOTS, LANES), jnp.float32),
            ],
        ),
        name="analysis",
    )(where, model, driver, rows, columns)


def synthesis(where, model, own, sibling, rate, cap, rows, columns, cells):
    fields, height, width = model.shape
    steps = fields // BLOCK
    groups = fields // GROUP

    def at(s, w):
        return ((s + w[2] * (steps // 2)) % steps, 0, 0)

    def group_at(s, w):
        return ((s // 2 + w[2] * (groups // 2)) % groups, 0, 0)

    block = pl.BlockSpec((BLOCK, height, width), at)
    whole = pl.BlockSpec(own.shape, lambda s, w: (0, 0))
    limits = pl.BlockSpec((1, SLOTS, LANES), group_at)
    return pl.pallas_call(
        lambda *refs: synthesis_kernel(cells, *refs),
        out_shape=jax.ShapeDtypeStruct(model.shape, jnp.float32),
        grid_spec=pltpu.PrefetchScalarGridSpec(
            num_scalar_prefetch=1,
            grid=(steps,),
            in_specs=[
                block,
                whole,
                whole,
                limits,
                limits,
                pl.BlockSpec((1, *rows.shape[1:]), lambda s, w: (w[0], 0, 0)),
                pl.BlockSpec((1, *columns.shape[1:]), lambda s, w: (w[1], 0, 0)),
            ],
            out_specs=block,
            scratch_shapes=[
                pltpu.VMEM((TILES * LANES, LANES), jnp.float32),
                pltpu.VMEM((SLOTS, LANES), jnp.float32),
            ],
        ),
        name="synthesis",
    )(where, model, own, sibling, rate, cap, rows, columns)


def per_group(value):
    rows = value.reshape(-1, GROUP, 1)
    rows = jnp.pad(rows, ((0, 0), (0, SLOTS - GROUP), (0, 0)), constant_values=1.0)
    return jnp.broadcast_to(rows, (rows.shape[0], SLOTS, LANES))


def per_device(model_field, driver_field, nudge_rate, increment_cap):
    fields, height, width = model_field.shape
    parts_y = lax.axis_size(("x", "c"))
    parts_x = lax.axis_size(("z", "y"))
    chips = lax.axis_size(CHIP)
    swap = [(0, 1), (1, 0)]
    where = jnp.stack(
        [lax.axis_index(("x", "c")), lax.axis_index(("z", "y")), lax.axis_index("c")]
    ).astype(jnp.int32)

    high_y, low_y = split_table(height * parts_y, parts_y)
    high_x, low_x = split_table(width * parts_x, parts_x)
    turned = lambda table: np.swapaxes(table, 1, 2)
    rows_in = np.concatenate([turned(high_y), turned(low_y)], axis=1)
    columns_in = np.concatenate([turned(high_x), turned(low_x)], axis=1)
    columns_in = np.concatenate([columns_in, columns_in], axis=2)
    rows_out = np.concatenate([high_y, high_y, low_y], axis=2)
    columns_out = np.concatenate([turned(high_x), turned(low_x)], axis=2)

    mine, other = analysis(where, model_field, driver_field, rows_in, columns_in)
    pair = mine + lax.ppermute(other, "c", swap)
    pieces = lax.all_to_all(pair.reshape(chips, 1, -1), CHIP, 0, 0, tiled=True)
    piece = jnp.sum(pieces, axis=0, keepdims=True)
    own = lax.all_to_all(jnp.broadcast_to(piece, pieces.shape), CHIP, 0, 0, tiled=True)
    own = own.reshape(mine.shape)
    sibling = lax.ppermute(own, "c", swap)
    cells = height * parts_y * width * parts_x
    return synthesis(
        where,
        model_field,
        own,
        sibling,
        per_group(nudge_rate),
        per_group(increment_cap),
        rows_out,
        columns_out,
        float(cells),
    )


def solution(mesh):
    finer = Mesh(mesh.devices.reshape(4, 2, 4, 4), ("x", "c", "z", "y"))
    field = P(None, ("x", "c"), ("z", "y"))
    return jax.shard_map(
        per_device,
        mesh=finer,
        in_specs=(field, field, P(), P()),
        out_specs=field,
        check_vma=False,
    )
```

```python
import numpy as np

import jax
import jax.numpy as jnp
import ml_dtypes
from jax import lax
from jax.experimental import pallas as pl
from jax.experimental.pallas import tpu as pltpu
from jax.sharding import Mesh
from jax.sharding import PartitionSpec as P

MODES = 24
WAVES = 2 * MODES
GROUP = 10
TILES = 4
LANES = 128
SLOTS = 16
CHIP = ("x", "z", "y")
EPSILON = 1e-06


def basis_table(length):
    positions = np.arange(length)
    wavenumber = np.concatenate([np.arange(MODES), np.arange(MODES) + 1])
    phases = positions[:, None] * wavenumber[None, :] % length
    angles = phases * (2.0 * np.pi / length)
    column = np.arange(WAVES)
    weights = np.where(column == 0, np.sqrt(1.0 / length), np.sqrt(2.0 / length))
    return np.where(column[None, :] < MODES, np.cos(angles), np.sin(angles)) * weights[None, :]


def split_table(length, parts):
    table = basis_table(length).astype(np.float32)
    high = table.astype(ml_dtypes.bfloat16)
    low = (table - high.astype(np.float32)).astype(ml_dtypes.bfloat16)
    shape = (parts, length // parts, WAVES)
    return high.reshape(shape), low.reshape(shape)


def split(value):
    high = value.astype(jnp.bfloat16)
    low = (value - high.astype(jnp.float32)).astype(jnp.bfloat16)
    return high, low


def dot(left, right, contract):
    return lax.dot_general(left, right, (contract, ((), ())), preferred_element_type=jnp.float32)


def analysis_kernel(
    model_hbm, driver_hbm, rows_hbm, columns_hbm, mine, other, model,
    driver, rows, columns, along_y, squares, arrived, ready,
):
    gy, gx, core = lax.axis_index(("x", "c")), lax.axis_index(("z", "y")), lax.axis_index("c")
    groups = model.shape[0] // GROUP
    tables = [
        pltpu.make_async_copy(rows_hbm.at[gy], rows, ready.at[0]),
        pltpu.make_async_copy(columns_hbm.at[gx], columns, ready.at[1]),
    ]

    def chunks(group):
        span = pl.ds(group * GROUP, GROUP)
        return [
            pltpu.make_async_copy(model_hbm.at[span], model.at[span], arrived.at[0, group]),
            pltpu.make_async_copy(driver_hbm.at[span], driver.at[span], arrived.at[1, group]),
        ]

    for copy in tables:
        copy.start()
    for group in range(groups):
        for copy in chunks(group):
            copy.start()
    along_y[...] = jnp.zeros_like(along_y)
    squares[...] = jnp.zeros_like(squares)
    for copy in tables:
        copy.wait()

    def one_group(group, carry):
        for copy in chunks(group):
            copy.wait()
        for i in range(GROUP):
            field = group * GROUP + i
            difference = driver[field] - model[field]
            squares[i : i + 1, :] = jnp.sum(difference * difference, axis=0, keepdims=True)
            parts = jnp.concatenate(split(difference), axis=1)
            product = dot(rows[...], parts, ((1,), (0,)))
            product = product[:WAVES] + product[WAVES:]
            high, low = split(product[:, :LANES] + product[:, LANES:])
            along_y[i * WAVES : (i + 1) * WAVES, :LANES] = high
            along_y[i * WAVES : (i + 1) * WAVES, LANES:] = low
        both = dot(columns[...], along_y[...], ((1,), (1,)))
        both = both[:WAVES] + both[WAVES:]
        tiles = [both[:, t * LANES : (t + 1) * LANES] for t in range(TILES)]
        total = jnp.sum(squares[...], axis=1, keepdims=True)
        lane = lax.broadcasted_iota(jnp.int32, (SLOTS, LANES), 1)
        top = jnp.where(lane == LANES - 1, total, tiles[-1][:SLOTS])
        tiles[-1] = jnp.concatenate([top, tiles[-1][SLOTS:]], axis=0)
        first = pl.multiple_of((group % (groups // 2)) * (TILES * WAVES), 8)

        def keep(ref):
            for t in range(TILES):
                ref[pl.ds(first + t * WAVES, WAVES), :] = tiles[t]

        half = group // (groups // 2)
        pl.when(half == core)(lambda: keep(mine))
        pl.when(half != core)(lambda: keep(other))
        return carry

    lax.fori_loop(0, groups, one_group, 0)


def synthesis_kernel(
    cells, own, sibling, rate, cap, model, rows_hbm, columns_hbm, nudged_hbm,
    nudged, rows, columns, along_x, spread, leaving, ready,
):
    gy, gx, core = lax.axis_index(("x", "c")), lax.axis_index(("z", "y")), lax.axis_index("c")
    groups = model.shape[0] // GROUP
    tables = [
        pltpu.make_async_copy(rows_hbm.at[gy], rows, ready.at[0]),
        pltpu.make_async_copy(columns_hbm.at[gx], columns, ready.at[1]),
    ]

    def ordered(step):
        return lax.rem(step + core * (groups // 2), groups)

    def chunk_out(group):
        span = pl.ds(group * GROUP, GROUP)
        return pltpu.make_async_copy(nudged.at[span], nudged_hbm.at[span], leaving.at[group])

    for copy in tables:
        copy.start()
    for copy in tables:
        copy.wait()

    def one_group(step, carry):
        group = ordered(step)

        def prepare(ref):
            first = pl.multiple_of((step % (groups // 2)) * (TILES * WAVES), 8)
            tiles = [ref[pl.ds(first + t * WAVES, WAVES), :] for t in range(TILES)]
            total = tiles[-1][:SLOTS, LANES - 1 :]
            spread[...] = jnp.broadcast_to(jnp.sqrt(total / cells + EPSILON), spread.shape)
            high, low = split(jnp.concatenate(tiles, axis=1))
            both = dot(high, columns[...], ((0,), (0,))) + dot(low, columns[...], ((0,), (0,)))
            along_x[...] = both[:, :LANES] + both[:, LANES:]

        pl.when(step < groups // 2)(lambda: prepare(own))
        pl.when(step >= groups // 2)(lambda: prepare(sibling))
        for i in range(0, GROUP, 2):
            stacks = []
            for j in (i, i + 1):
                field = group * GROUP + j
                strength = rate[field] * jnp.minimum(1.0, cap[field] / spread[j : j + 1, :])
                high, low = split(along_x[j * WAVES : (j + 1) * WAVES, :] * strength)
                stacks.append(jnp.concatenate([high, low, high], axis=0))
            pair = dot(rows[...], jnp.concatenate(stacks, axis=1), ((1,), (0,)))
            for j in (0, 1):
                field = group * GROUP + i + j
                nudged[field] = model[field] + pair[:, j * LANES : (j + 1) * LANES]
        chunk_out(group).start()
        return carry

    lax.fori_loop(0, groups, one_group, 0)
    for group in range(groups):
        chunk_out(group).wait()


IN_HBM = pl.BlockSpec(memory_space=pltpu.HBM)
IN_VMEM = pl.BlockSpec(memory_space=pltpu.VMEM)
IN_SMEM = pl.BlockSpec(memory_space=pltpu.SMEM)


def share_kernel(chips, pieces, copies, rows):
    height = pieces.shape[0] // chips
    period = 8 * height
    total = pieces[:period, :]
    for first in range(period, pieces.shape[0], period):
        total = total + pieces[first : first + period, :]
    rows[...] = total
    for i in range(height):
        every = pl.ds(i, 8, stride=height)
        line = jnp.sum(rows[every, :], axis=0, keepdims=True)
        rows[every, :] = jnp.broadcast_to(line, (8, LANES))
    for first in range(0, pieces.shape[0], period):
        copies[first : first + period, :] = rows[...]


def share(pieces, chips):
    return pl.pallas_call(
        lambda *refs: share_kernel(chips, *refs),
        out_shape=pltpu.VMEM(pieces.shape, jnp.float32),
        in_specs=[IN_VMEM],
        out_specs=IN_VMEM,
        scratch_shapes=[pltpu.VMEM((8 * pieces.shape[0] // chips, LANES), jnp.float32)],
        compiler_params=pltpu.CompilerParams(vmem_limit_bytes=2 << 20),
        name="share",
    )(kept_in_vmem(pieces))


def kept_in_hbm(value):
    return pltpu.with_memory_space_constraint(value, pltpu.HBM)


def kept_in_vmem(value):
    return pltpu.with_memory_space_constraint(value, pltpu.VMEM)


def analysis(model, driver, rows, columns):
    groups = model.shape[0] // GROUP
    half = groups // 2 * TILES * WAVES
    return pl.pallas_call(
        analysis_kernel,
        out_shape=[
            pltpu.VMEM((half, LANES), jnp.float32),
            pltpu.VMEM((half, LANES), jnp.float32),
            pltpu.VMEM(model.shape, jnp.float32),
        ],
        in_specs=[IN_HBM] * 4,
        out_specs=[IN_VMEM] * 3,
        scratch_shapes=[
            pltpu.VMEM(model.shape, jnp.float32),
            pltpu.VMEM(rows.shape[1:], jnp.bfloat16),
            pltpu.VMEM(columns.shape[1:], jnp.bfloat16),
            pltpu.VMEM((TILES * LANES, 2 * LANES), jnp.bfloat16),
            pltpu.VMEM((SLOTS, LANES), jnp.float32),
            pltpu.SemaphoreType.DMA((2, groups)),
            pltpu.SemaphoreType.DMA((2,)),
        ],
        compiler_params=pltpu.CompilerParams(vmem_limit_bytes=24 << 20),
        name="analysis",
    )(*map(kept_in_hbm, (model, driver, rows, columns)))


def synthesis(model, own, sibling, rate, cap, rows, columns, cells):
    groups = model.shape[0] // GROUP
    return pl.pallas_call(
        lambda *refs: synthesis_kernel(cells, *refs),
        out_shape=pltpu.HBM(model.shape, jnp.float32),
        in_specs=[IN_VMEM] * 2 + [IN_SMEM] * 2 + [IN_VMEM] + [IN_HBM] * 2,
        out_specs=IN_HBM,
        scratch_shapes=[
            pltpu.VMEM(model.shape, jnp.float32),
            pltpu.VMEM(rows.shape[1:], jnp.bfloat16),
            pltpu.VMEM(columns.shape[1:], jnp.bfloat16),
            pltpu.VMEM((TILES * LANES, LANES), jnp.float32),
            pltpu.VMEM((SLOTS, LANES), jnp.float32),
            pltpu.SemaphoreType.DMA((groups,)),
            pltpu.SemaphoreType.DMA((2,)),
        ],
        compiler_params=pltpu.CompilerParams(vmem_limit_bytes=24 << 20),
        name="synthesis",
    )(
        kept_in_vmem(own),
        kept_in_vmem(sibling),
        rate,
        cap,
        kept_in_vmem(model),
        kept_in_hbm(rows),
        kept_in_hbm(columns),
    )


def per_device(model_field, driver_field, nudge_rate, increment_cap):
    fields, height, width = model_field.shape
    parts_y = lax.axis_size(("x", "c"))
    parts_x = lax.axis_size(("z", "y"))
    chips = lax.axis_size(CHIP)
    swap = [(0, 1), (1, 0)]

    high_y, low_y = split_table(height * parts_y, parts_y)
    high_x, low_x = split_table(width * parts_x, parts_x)
    turned = lambda table: np.swapaxes(table, 1, 2)
    rows_in = np.concatenate([turned(high_y), turned(low_y)], axis=1)
    columns_in = np.concatenate([turned(high_x), turned(low_x)], axis=1)
    columns_in = np.concatenate([columns_in, columns_in], axis=2)
    rows_out = np.concatenate([high_y, high_y, low_y], axis=2)
    columns_out = np.concatenate([turned(high_x), turned(low_x)], axis=2)

    mine, other, model_kept = analysis(model_field, driver_field, rows_in, columns_in)
    pair = mine + lax.ppermute(other, "c", swap)

    def exchanged(value):
        blocks = value.reshape(chips, 1, -1)
        return lax.all_to_all(blocks, CHIP, 0, 0, tiled=True).reshape(value.shape)

    own = exchanged(share(exchanged(pair), chips))
    sibling = lax.ppermute(own, "c", swap)
    cells = height * parts_y * width * parts_x
    return synthesis(
        model_kept,
        own,
        sibling,
        nudge_rate,
        increment_cap,
        rows_out,
        columns_out,
        float(cells),
    )


def solution(mesh):
    finer = Mesh(mesh.devices.reshape(4, 2, 4, 4), ("x", "c", "z", "y"))
    field = P(None, ("x", "c"), ("z", "y"))
    return jax.shard_map(
        per_device,
        mesh=finer,
        in_specs=(field, field, P(), P()),
        out_specs=field,
        check_vma=False,
    )
```

```python
import numpy as np

import jax
import jax.numpy as jnp
import ml_dtypes
from jax import lax
from jax.experimental import pallas as pl
from jax.experimental.pallas import tpu as pltpu
from jax.sharding import Mesh
from jax.sharding import PartitionSpec as P

MODES = 24
WAVES = 2 * MODES
GROUP = 10
TILES = 4
LANES = 128
AHEAD = 3
LAST_PIECES = (6, 4)
CHUNK = 10
SLOTS = 16
CHIP = ("x", "z", "y")
EPSILON = 1e-06


def basis_table(length):
    positions = np.arange(length)
    wavenumber = np.concatenate([np.arange(MODES), np.arange(MODES) + 1])
    phases = positions[:, None] * wavenumber[None, :] % length
    angles = phases * (2.0 * np.pi / length)
    column = np.arange(WAVES)
    weights = np.where(column == 0, np.sqrt(1.0 / length), np.sqrt(2.0 / length))
    return np.where(column[None, :] < MODES, np.cos(angles), np.sin(angles)) * weights[None, :]


def split_table(length, parts):
    table = basis_table(length).astype(np.float32)
    high = table.astype(ml_dtypes.bfloat16)
    low = (table - high.astype(np.float32)).astype(ml_dtypes.bfloat16)
    shape = (parts, length // parts, WAVES)
    return high.reshape(shape), low.reshape(shape)


def split(value):
    high = value.astype(jnp.bfloat16)
    low = (value - high.astype(jnp.float32)).astype(jnp.bfloat16)
    return high, low


def dot(left, right, contract):
    return lax.dot_general(left, right, (contract, ((), ())), preferred_element_type=jnp.float32)


def analysis_kernel(
    model_hbm, driver_hbm, rate_hbm, cap_hbm, rows_hbm, columns_hbm, rows_out_hbm, columns_out_hbm,
    mine, other, model, rate_rows, cap_rows, rows_out, columns_out,
    driver, rate, cap, rows, columns, along_y, squares, arrived, ready,
):
    gy, gx, core = lax.axis_index(("x", "c")), lax.axis_index(("z", "y")), lax.axis_index("c")
    groups = model.shape[0] // GROUP
    tables = [
        pltpu.make_async_copy(rows_hbm.at[gy], rows, ready.at[0]),
        pltpu.make_async_copy(columns_hbm.at[gx], columns, ready.at[1]),
    ]
    later = [
        pltpu.make_async_copy(rate_hbm, rate, ready.at[2]),
        pltpu.make_async_copy(cap_hbm, cap, ready.at[3]),
        pltpu.make_async_copy(rows_out_hbm.at[gy], rows_out, ready.at[4]),
        pltpu.make_async_copy(columns_out_hbm.at[gx], columns_out, ready.at[5]),
    ]

    def ordered(step):
        return lax.rem(step + (1 - core) * (groups // 2), groups)

    pieces = []
    for step in range(groups):
        sizes = LAST_PIECES if step == groups - 1 else (GROUP,)
        first = 0
        for size in sizes:
            pieces.append((step, first, size))
            first += size

    def fetch(piece):
        step, first, size = pieces[piece]
        span = pl.ds(ordered(step) * GROUP + first, size)
        return [
            pltpu.make_async_copy(model_hbm.at[span], model.at[span], arrived.at[0, piece]),
            pltpu.make_async_copy(driver_hbm.at[span], driver.at[span], arrived.at[1, piece]),
        ]

    for copy in tables + fetch(0) + later:
        copy.start()
    for piece in range(1, AHEAD):
        for copy in fetch(piece):
            copy.start()
    along_y[...] = jnp.zeros_like(along_y)
    squares[...] = jnp.zeros_like(squares)

    def first_contraction(step, i):
        field = ordered(step) * GROUP + i
        difference = driver[field] - model[field]
        folded = (difference * difference).reshape(-1, 8, LANES)
        squares[step % 2, i * 8 : i * 8 + 8, :] = jnp.sum(folded, axis=0)
        parts = jnp.concatenate(split(difference), axis=1)
        product = dot(rows[...], parts, ((1,), (0,)))
        product = product[:WAVES] + product[WAVES:]
        high, low = split(product[:, :LANES] + product[:, LANES:])
        along_y[step % 2, i * WAVES : (i + 1) * WAVES, :LANES] = high
        along_y[step % 2, i * WAVES : (i + 1) * WAVES, LANES:] = low

    def second_contraction(step):
        both = dot(columns[...], along_y[step % 2], ((1,), (1,)))
        both = both[:WAVES] + both[WAVES:]
        total = squares[step % 2, pl.ds(0, SLOTS, stride=8), :]
        for s in range(1, 8):
            total = total + squares[step % 2, pl.ds(s, SLOTS, stride=8), :]
        total = jnp.sum(total, axis=1, keepdims=True)
        tiles = [both[:, t * LANES : (t + 1) * LANES] for t in range(TILES)]
        lane = lax.broadcasted_iota(jnp.int32, (SLOTS, LANES), 1)
        top = jnp.where(lane == LANES - 1, total, tiles[-1][:SLOTS])
        tiles[-1] = jnp.concatenate([top, tiles[-1][SLOTS:]], axis=0)
        kept = other if step < groups // 2 else mine
        first = step % (groups // 2) * TILES * WAVES
        for t in range(TILES):
            kept[first + t * WAVES : first + (t + 1) * WAVES, :] = tiles[t]

    for piece, (step, first, size) in enumerate(pieces):
        if piece == 0:
            for copy in tables:
                copy.wait()
        for copy in fetch(piece):
            copy.wait()
        if piece + AHEAD < len(pieces):
            for copy in fetch(piece + AHEAD):
                copy.start()
        for i in range(first, first + size):
            first_contraction(step, i)
            if i == 2 and step > 0:
                second_contraction(step - 1)
        if step == 1:
            for copy in later:
                copy.wait()
            for field in range(model.shape[0]):
                place = field // GROUP * SLOTS + field % GROUP
                rate_rows[place : place + 1, :] = jnp.full((1, LANES), rate[field])
                cap_rows[place : place + 1, :] = jnp.full((1, LANES), cap[field])
    second_contraction(groups - 1)


def synthesis_kernel(
    cells, own, sibling, rate_rows, cap_rows, model, rows, columns, nudged_hbm,
    nudged, along_x, strength, leaving,
):
    core = lax.axis_index("c")
    groups = model.shape[0] // GROUP

    def ordered(step):
        return lax.rem(step + core * (groups // 2), groups)

    def chunk_out(step, first, size):
        span = pl.ds(ordered(step) * GROUP + first, size)
        place = leaving.at[step * (GROUP // CHUNK) + first // CHUNK]
        return pltpu.make_async_copy(nudged.at[span], nudged_hbm.at[span], place)

    def prepare(step):
        ref = own if step < groups // 2 else sibling
        first = step % (groups // 2) * TILES * WAVES
        tiles = [ref[first + t * WAVES : first + (t + 1) * WAVES, :] for t in range(TILES)]
        limits = pl.ds(pl.multiple_of(ordered(step) * SLOTS, SLOTS), SLOTS)
        spread = jnp.sqrt(tiles[-1][:SLOTS, LANES - 1 :] / cells + EPSILON)
        strength[step % 2] = rate_rows[limits, :] * jnp.minimum(1.0, cap_rows[limits, :] / spread)
        high, low = split(jnp.concatenate(tiles, axis=1))
        both = dot(high, columns[...], ((0,), (0,))) + dot(low, columns[...], ((0,), (0,)))
        along_x[step % 2] = both[:, :LANES] + both[:, LANES:]

    prepare(0)
    for step in range(groups):
        for i in range(0, GROUP, 2):
            stacks = []
            for j in (i, i + 1):
                scaled = along_x[step % 2, j * WAVES : (j + 1) * WAVES, :]
                high, low = split(scaled * strength[step % 2, j : j + 1, :])
                stacks.append(jnp.concatenate([high, low, high], axis=0))
            pair = dot(rows[...], jnp.concatenate(stacks, axis=1), ((1,), (0,)))
            for j in (0, 1):
                field = ordered(step) * GROUP + i + j
                nudged[field] = model[field] + pair[:, j * LANES : (j + 1) * LANES]
            if i == 0 and step + 1 < groups:
                prepare(step + 1)
            if (i + 2) % CHUNK == 0:
                chunk_out(step, i + 2 - CHUNK, CHUNK).start()
    for step in range(groups):
        for first in range(0, GROUP, CHUNK):
            chunk_out(step, first, CHUNK).wait()


IN_HBM = pl.BlockSpec(memory_space=pltpu.HBM)
IN_VMEM = pl.BlockSpec(memory_space=pltpu.VMEM)
IN_SMEM = pl.BlockSpec(memory_space=pltpu.SMEM)


def share_kernel(chips, pieces, copies, rows):
    height = pieces.shape[0] // chips
    period = 8 * height
    total = pieces[:period, :]
    for first in range(period, pieces.shape[0], period):
        total = total + pieces[first : first + period, :]
    rows[...] = total
    for i in range(height):
        every = pl.ds(i, 8, stride=height)
        line = jnp.sum(rows[every, :], axis=0, keepdims=True)
        rows[every, :] = jnp.broadcast_to(line, (8, LANES))
    for first in range(0, pieces.shape[0], period):
        copies[first : first + period, :] = rows[...]


def share(pieces, chips):
    return pl.pallas_call(
        lambda *refs: share_kernel(chips, *refs),
        out_shape=pltpu.VMEM(pieces.shape, jnp.float32),
        in_specs=[IN_VMEM],
        out_specs=IN_VMEM,
        scratch_shapes=[pltpu.VMEM((8 * pieces.shape[0] // chips, LANES), jnp.float32)],
        compiler_params=pltpu.CompilerParams(vmem_limit_bytes=2 << 20),
        name="share",
    )(kept_in_vmem(pieces))


def kept_in_hbm(value):
    return pltpu.with_memory_space_constraint(value, pltpu.HBM)


def kept_in_vmem(value):
    return pltpu.with_memory_space_constraint(value, pltpu.VMEM)


def analysis(model, driver, rate, cap, rows, columns, rows_out, columns_out):
    groups = model.shape[0] // GROUP
    half = groups // 2 * TILES * WAVES
    pieces = groups - 1 + len(LAST_PIECES)
    return pl.pallas_call(
        analysis_kernel,
        out_shape=[
            pltpu.VMEM((half, LANES), jnp.float32),
            pltpu.VMEM((half, LANES), jnp.float32),
            pltpu.VMEM(model.shape, jnp.float32),
            pltpu.VMEM((groups * SLOTS, LANES), jnp.float32),
            pltpu.VMEM((groups * SLOTS, LANES), jnp.float32),
            pltpu.VMEM(rows_out.shape[1:], jnp.bfloat16),
            pltpu.VMEM(columns_out.shape[1:], jnp.bfloat16),
        ],
        in_specs=[IN_HBM] * 8,
        out_specs=[IN_VMEM] * 7,
        scratch_shapes=[
            pltpu.VMEM(model.shape, jnp.float32),
            pltpu.SMEM(rate.shape, jnp.float32),
            pltpu.SMEM(cap.shape, jnp.float32),
            pltpu.VMEM(rows.shape[1:], jnp.bfloat16),
            pltpu.VMEM(columns.shape[1:], jnp.bfloat16),
            pltpu.VMEM((2, TILES * LANES, 2 * LANES), jnp.bfloat16),
            pltpu.VMEM((2, 8 * SLOTS, LANES), jnp.float32),
            pltpu.SemaphoreType.DMA((2, pieces)),
            pltpu.SemaphoreType.DMA((6,)),
        ],
        compiler_params=pltpu.CompilerParams(vmem_limit_bytes=24 << 20),
        name="analysis",
    )(*map(kept_in_hbm, (model, driver, rate, cap, rows, columns, rows_out, columns_out)))


def synthesis(own, sibling, rate_rows, cap_rows, model, rows, columns, cells):
    groups = model.shape[0] // GROUP
    return pl.pallas_call(
        lambda *refs: synthesis_kernel(cells, *refs),
        out_shape=pltpu.HBM(model.shape, jnp.float32),
        in_specs=[IN_VMEM] * 7,
        out_specs=IN_HBM,
        scratch_shapes=[
            pltpu.VMEM(model.shape, jnp.float32),
            pltpu.VMEM((2, TILES * LANES, LANES), jnp.float32),
            pltpu.VMEM((2, SLOTS, LANES), jnp.float32),
            pltpu.SemaphoreType.DMA((groups * (GROUP // CHUNK),)),
        ],
        compiler_params=pltpu.CompilerParams(vmem_limit_bytes=24 << 20),
        name="synthesis",
    )(*map(kept_in_vmem, (own, sibling, rate_rows, cap_rows, model, rows, columns)))


def per_device(model_field, driver_field, nudge_rate, increment_cap):
    fields, height, width = model_field.shape
    parts_y = lax.axis_size(("x", "c"))
    parts_x = lax.axis_size(("z", "y"))
    chips = lax.axis_size(CHIP)
    swap = [(0, 1), (1, 0)]

    high_y, low_y = split_table(height * parts_y, parts_y)
    high_x, low_x = split_table(width * parts_x, parts_x)
    turned = lambda table: np.swapaxes(table, 1, 2)
    rows_in = np.concatenate([turned(high_y), turned(low_y)], axis=1)
    columns_in = np.concatenate([turned(high_x), turned(low_x)], axis=1)
    columns_in = np.concatenate([columns_in, columns_in], axis=2)
    rows_out = np.concatenate([high_y, high_y, low_y], axis=2)
    columns_out = np.concatenate([turned(high_x), turned(low_x)], axis=2)

    mine, other, *kept = analysis(
        model_field,
        driver_field,
        nudge_rate,
        increment_cap,
        rows_in,
        columns_in,
        rows_out,
        columns_out,
    )
    model_kept, rate_rows, cap_rows, rows_kept, columns_kept = kept
    pair = mine + lax.ppermute(other, "c", swap)

    def exchanged(value):
        blocks = value.reshape(chips, 1, -1)
        return lax.all_to_all(blocks, CHIP, 0, 0, tiled=True).reshape(value.shape)

    own = exchanged(share(exchanged(pair), chips))
    sibling = lax.ppermute(own, "c", swap)
    cells = float(height * parts_y * width * parts_x)
    return synthesis(
        own, sibling, rate_rows, cap_rows, model_kept, rows_kept, columns_kept, cells
    )


def solution(mesh):
    finer = Mesh(mesh.devices.reshape(4, 2, 4, 4), ("x", "c", "z", "y"))
    field = P(None, ("x", "c"), ("z", "y"))
    return jax.shard_map(
        per_device,
        mesh=finer,
        in_specs=(field, field, P(), P()),
        out_specs=field,
        check_vma=False,
    )
```

```python
import numpy as np

import jax
import jax.numpy as jnp
import ml_dtypes
from jax import lax
from jax.experimental import pallas as pl
from jax.experimental.pallas import tpu as pltpu
from jax.sharding import Mesh
from jax.sharding import PartitionSpec as P

MODES = 24
WAVES = 2 * MODES
GROUP = 10
TILES = 4
LANES = 128
AHEAD = 3
LAST_PIECES = (6, 4)
CHUNK = 10
SLOTS = 16
CHIP = ("x", "z", "y")
EPSILON = 1e-06


def basis_table(length):
    positions = np.arange(length)
    wavenumber = np.concatenate([np.arange(MODES), np.arange(MODES) + 1])
    phases = positions[:, None] * wavenumber[None, :] % length
    angles = phases * (2.0 * np.pi / length)
    column = np.arange(WAVES)
    weights = np.where(column == 0, np.sqrt(1.0 / length), np.sqrt(2.0 / length))
    return np.where(column[None, :] < MODES, np.cos(angles), np.sin(angles)) * weights[None, :]


def split_table(length, parts):
    table = basis_table(length).astype(np.float32)
    high = table.astype(ml_dtypes.bfloat16)
    low = (table - high.astype(np.float32)).astype(ml_dtypes.bfloat16)
    shape = (parts, length // parts, WAVES)
    return high.reshape(shape), low.reshape(shape)


def split(value):
    high = value.astype(jnp.bfloat16)
    low = (value - high.astype(jnp.float32)).astype(jnp.bfloat16)
    return high, low


def dot(left, right, contract):
    return lax.dot_general(left, right, (contract, ((), ())), preferred_element_type=jnp.float32)


def second_contraction(columns, along_y, squares, coefficients, step):
    both = dot(columns[...], along_y[...], ((1,), (1,)))
    both = both[:WAVES] + both[WAVES:]
    total = squares[pl.ds(0, SLOTS, stride=8), :]
    for s in range(1, 8):
        total = total + squares[pl.ds(s, SLOTS, stride=8), :]
    total = jnp.sum(total, axis=1, keepdims=True)
    tiles = [both[:, t * LANES : (t + 1) * LANES] for t in range(TILES)]
    lane = lax.broadcasted_iota(jnp.int32, (SLOTS, LANES), 1)
    top = jnp.where(lane == LANES - 1, total, tiles[-1][:SLOTS])
    tiles[-1] = jnp.concatenate([top, tiles[-1][SLOTS:]], axis=0)
    first = step * TILES * WAVES
    for t in range(TILES):
        coefficients[first + t * WAVES : first + (t + 1) * WAVES, :] = tiles[t]


def analysis_kernel(
    model_hbm, driver_hbm, rate_hbm, cap_hbm, rows_hbm, columns_hbm, rows_out_hbm, columns_out_hbm,
    other, along_own, squares_own, columns, model, rate_rows, cap_rows, rows_out, columns_out,
    driver, rate, cap, rows, along_y, squares, arrived, ready,
):
    gy, gx, core = lax.axis_index(("x", "c")), lax.axis_index(("z", "y")), lax.axis_index("c")
    groups = model.shape[0] // GROUP
    half = groups // 2
    tables = [
        pltpu.make_async_copy(rows_hbm.at[gy], rows, ready.at[0]),
        pltpu.make_async_copy(columns_hbm.at[gx], columns, ready.at[1]),
    ]
    later = [
        pltpu.make_async_copy(rate_hbm, rate, ready.at[2]),
        pltpu.make_async_copy(cap_hbm, cap, ready.at[3]),
        pltpu.make_async_copy(rows_out_hbm.at[gy], rows_out, ready.at[4]),
        pltpu.make_async_copy(columns_out_hbm.at[gx], columns_out, ready.at[5]),
    ]

    def ordered(step):
        return lax.rem(step + (1 - core) * half, groups)

    def held(step):
        if step < half:
            return along_y.at[step % 2], squares.at[step % 2]
        return along_own.at[step - half], squares_own.at[step - half]

    pieces = []
    for step in range(groups):
        sizes = LAST_PIECES if step == groups - 1 else (GROUP,)
        first = 0
        for size in sizes:
            pieces.append((step, first, size))
            first += size

    def fetch(piece):
        step, first, size = pieces[piece]
        span = pl.ds(ordered(step) * GROUP + first, size)
        return [
            pltpu.make_async_copy(model_hbm.at[span], model.at[span], arrived.at[0, piece]),
            pltpu.make_async_copy(driver_hbm.at[span], driver.at[span], arrived.at[1, piece]),
        ]

    for copy in tables + fetch(0) + later:
        copy.start()
    for piece in range(1, AHEAD):
        for copy in fetch(piece):
            copy.start()
    for step in [0, 1, *range(half, groups)]:
        lines, sums = held(step)
        lines[GROUP * WAVES :, :] = jnp.zeros((TILES * LANES - GROUP * WAVES, 2 * LANES), lines.dtype)
        sums[GROUP * 8 :, :] = jnp.zeros((8 * (SLOTS - GROUP), LANES), jnp.float32)

    def first_contraction(step, i):
        lines, sums = held(step)
        field = ordered(step) * GROUP + i
        difference = driver[field] - model[field]
        folded = (difference * difference).reshape(-1, 8, LANES)
        sums[i * 8 : i * 8 + 8, :] = jnp.sum(folded, axis=0)
        parts = jnp.concatenate(split(difference), axis=1)
        product = dot(rows[...], parts, ((1,), (0,)))
        product = product[:WAVES] + product[WAVES:]
        high, low = split(product[:, :LANES] + product[:, LANES:])
        lines[i * WAVES : (i + 1) * WAVES, :LANES] = high
        lines[i * WAVES : (i + 1) * WAVES, LANES:] = low

    for piece, (step, first, size) in enumerate(pieces):
        if piece == 0:
            for copy in tables:
                copy.wait()
        for copy in fetch(piece):
            copy.wait()
        if piece + AHEAD < len(pieces):
            for copy in fetch(piece + AHEAD):
                copy.start()
        for i in range(first, first + size):
            first_contraction(step, i)
            if i == 2 and 0 < step <= half:
                second_contraction(columns, *held(step - 1), other, step - 1)
        if piece == 1:
            for copy in later:
                copy.wait()
            for field in range(model.shape[0]):
                place = field // GROUP * SLOTS + field % GROUP
                rate_rows[place : place + 1, :] = jnp.full((1, LANES), rate[field])
                cap_rows[place : place + 1, :] = jnp.full((1, LANES), cap[field])


def contract_kernel(along_own, squares_own, columns, mine):
    for step in range(along_own.shape[0]):
        second_contraction(columns, along_own.at[step], squares_own.at[step], mine, step)


def tiles_of(coefficients, step):
    first = step * TILES * WAVES
    return [coefficients[first + t * WAVES : first + (t + 1) * WAVES, :] for t in range(TILES)]


def strengths(cells, tiles, rate_rows, cap_rows, group):
    limits = pl.ds(pl.multiple_of(group * SLOTS, SLOTS), SLOTS)
    spread = jnp.sqrt(tiles[-1][:SLOTS, LANES - 1 :] / cells + EPSILON)
    return rate_rows[limits, :] * jnp.minimum(1.0, cap_rows[limits, :] / spread)


def synthesized(tiles, columns):
    high, low = split(jnp.concatenate(tiles, axis=1))
    both = dot(high, columns[...], ((0,), (0,))) + dot(low, columns[...], ((0,), (0,)))
    return both[:, :LANES] + both[:, LANES:]


def stacked(lines, strength):
    high, low = split(lines * strength)
    return jnp.concatenate([high, low, high], axis=0)


def begin_kernel(cells, own, rate_rows, cap_rows, columns, stacks):
    groups = own.shape[0] // (TILES * WAVES)
    base = lax.axis_index("c") * groups
    for step in range(groups):
        tiles = tiles_of(own, step)
        strength = strengths(cells, tiles, rate_rows, cap_rows, base + step)
        lines = synthesized(tiles, columns)
        for j in range(GROUP):
            stacks[step * GROUP + j] = stacked(
                lines[j * WAVES : (j + 1) * WAVES, :], strength[j : j + 1, :]
            )


def synthesis_kernel(
    cells, stacks, sibling, rate_rows, cap_rows, model, rows, columns, nudged_hbm,
    nudged, along_x, strength, leaving,
):
    core = lax.axis_index("c")
    groups = model.shape[0] // GROUP
    half = groups // 2

    def ordered(step):
        return lax.rem(step + core * half, groups)

    def chunk_out(step, first, size):
        span = pl.ds(ordered(step) * GROUP + first, size)
        place = leaving.at[step * (GROUP // CHUNK) + first // CHUNK]
        return pltpu.make_async_copy(nudged.at[span], nudged_hbm.at[span], place)

    def prepare(step):
        tiles = tiles_of(sibling, step - half)
        strength[step % 2] = strengths(cells, tiles, rate_rows, cap_rows, ordered(step))
        along_x[step % 2] = synthesized(tiles, columns)

    def stack_of(step, j):
        if step < half:
            return stacks[step * GROUP + j]
        lines = along_x[step % 2, j * WAVES : (j + 1) * WAVES, :]
        return stacked(lines, strength[step % 2, j : j + 1, :])

    for step in range(groups):
        for i in range(0, GROUP, 2):
            pair = jnp.concatenate([stack_of(step, i), stack_of(step, i + 1)], axis=1)
            pair = dot(rows[...], pair, ((1,), (0,)))
            for j in (0, 1):
                field = ordered(step) * GROUP + i + j
                nudged[field] = model[field] + pair[:, j * LANES : (j + 1) * LANES]
            if i == 0 and half <= step + 1 < groups:
                prepare(step + 1)
            if (i + 2) % CHUNK == 0:
                chunk_out(step, i + 2 - CHUNK, CHUNK).start()
    for step in range(groups):
        for first in range(0, GROUP, CHUNK):
            chunk_out(step, first, CHUNK).wait()


IN_HBM = pl.BlockSpec(memory_space=pltpu.HBM)
IN_VMEM = pl.BlockSpec(memory_space=pltpu.VMEM)
IN_SMEM = pl.BlockSpec(memory_space=pltpu.SMEM)


def share_kernel(chips, pieces, copies, rows):
    height = pieces.shape[0] // chips
    period = 8 * height
    total = pieces[:period, :]
    for first in range(period, pieces.shape[0], period):
        total = total + pieces[first : first + period, :]
    rows[...] = total
    for i in range(height):
        every = pl.ds(i, 8, stride=height)
        line = jnp.sum(rows[every, :], axis=0, keepdims=True)
        rows[every, :] = jnp.broadcast_to(line, (8, LANES))
    for first in range(0, pieces.shape[0], period):
        copies[first : first + period, :] = rows[...]


def share(pieces, chips):
    return pl.pallas_call(
        lambda *refs: share_kernel(chips, *refs),
        out_shape=pltpu.VMEM(pieces.shape, jnp.float32),
        in_specs=[IN_VMEM],
        out_specs=IN_VMEM,
        scratch_shapes=[pltpu.VMEM((8 * pieces.shape[0] // chips, LANES), jnp.float32)],
        compiler_params=pltpu.CompilerParams(vmem_limit_bytes=2 << 20),
        name="share",
    )(kept_in_vmem(pieces))


def kept_in_hbm(value):
    return pltpu.with_memory_space_constraint(value, pltpu.HBM)


def kept_in_vmem(value):
    return pltpu.with_memory_space_constraint(value, pltpu.VMEM)


def analysis(model, driver, rate, cap, rows, columns, rows_out, columns_out):
    groups = model.shape[0] // GROUP
    half = groups // 2
    pieces = groups - 1 + len(LAST_PIECES)
    lines = (TILES * LANES, 2 * LANES)
    sums = (8 * SLOTS, LANES)
    return pl.pallas_call(
        analysis_kernel,
        out_shape=[
            pltpu.VMEM((half * TILES * WAVES, LANES), jnp.float32),
            pltpu.VMEM((half, *lines), jnp.bfloat16),
            pltpu.VMEM((half, *sums), jnp.float32),
            pltpu.VMEM(columns.shape[1:], jnp.bfloat16),
            pltpu.VMEM(model.shape, jnp.float32),
            pltpu.VMEM((groups * SLOTS, LANES), jnp.float32),
            pltpu.VMEM((groups * SLOTS, LANES), jnp.float32),
            pltpu.VMEM(rows_out.shape[1:], jnp.bfloat16),
            pltpu.VMEM(columns_out.shape[1:], jnp.bfloat16),
        ],
        in_specs=[IN_HBM] * 8,
        out_specs=[IN_VMEM] * 9,
        scratch_shapes=[
            pltpu.VMEM(model.shape, jnp.float32),
            pltpu.SMEM(rate.shape, jnp.float32),
            pltpu.SMEM(cap.shape, jnp.float32),
            pltpu.VMEM(rows.shape[1:], jnp.bfloat16),
            pltpu.VMEM((2, *lines), jnp.bfloat16),
            pltpu.VMEM((2, *sums), jnp.float32),
            pltpu.SemaphoreType.DMA((2, pieces)),
            pltpu.SemaphoreType.DMA((6,)),
        ],
        compiler_params=pltpu.CompilerParams(vmem_limit_bytes=16 << 20),
        cost_estimate=estimate(2 * model.size),
        name="analysis",
    )(*map(kept_in_hbm, (model, driver, rate, cap, rows, columns, rows_out, columns_out)))


def contract(along_own, squares_own, columns):
    shape = (along_own.shape[0] * TILES * WAVES, LANES)
    return pl.pallas_call(
        contract_kernel,
        out_shape=pltpu.VMEM(shape, jnp.float32),
        in_specs=[IN_VMEM] * 3,
        out_specs=IN_VMEM,
        compiler_params=pltpu.CompilerParams(vmem_limit_bytes=2 << 20),
        cost_estimate=estimate(along_own.size),
        name="contract",
    )(*map(kept_in_vmem, (along_own, squares_own, columns)))


def begin(own, rate_rows, cap_rows, columns, cells):
    fields = own.shape[0] // (TILES * WAVES) * GROUP
    return pl.pallas_call(
        lambda *refs: begin_kernel(cells, *refs),
        out_shape=pltpu.VMEM((fields, 3 * WAVES, LANES), jnp.bfloat16),
        in_specs=[IN_VMEM] * 4,
        out_specs=IN_VMEM,
        compiler_params=pltpu.CompilerParams(vmem_limit_bytes=2 << 20),
        cost_estimate=estimate(fields * 3 * WAVES * LANES),
        name="begin",
    )(*map(kept_in_vmem, (own, rate_rows, cap_rows, columns)))


def synthesis(stacks, sibling, rate_rows, cap_rows, model, rows, columns, cells):
    groups = model.shape[0] // GROUP
    return pl.pallas_call(
        lambda *refs: synthesis_kernel(cells, *refs),
        out_shape=pltpu.HBM(model.shape, jnp.float32),
        in_specs=[IN_VMEM] * 7,
        out_specs=IN_HBM,
        scratch_shapes=[
            pltpu.VMEM(model.shape, jnp.float32),
            pltpu.VMEM((2, TILES * LANES, LANES), jnp.float32),
            pltpu.VMEM((2, SLOTS, LANES), jnp.float32),
            pltpu.SemaphoreType.DMA((groups * (GROUP // CHUNK),)),
        ],
        compiler_params=pltpu.CompilerParams(vmem_limit_bytes=12 << 20),
        cost_estimate=estimate(2 * model.size),
        name="synthesis",
    )(*map(kept_in_vmem, (stacks, sibling, rate_rows, cap_rows, model, rows, columns)))


def estimate(values):
    return pl.CostEstimate(flops=600 * values, bytes_accessed=4 * values, transcendentals=0)


def per_device(model_field, driver_field, nudge_rate, increment_cap):
    fields, height, width = model_field.shape
    parts_y = lax.axis_size(("x", "c"))
    parts_x = lax.axis_size(("z", "y"))
    chips = lax.axis_size(CHIP)
    swap = [(0, 1), (1, 0)]

    high_y, low_y = split_table(height * parts_y, parts_y)
    high_x, low_x = split_table(width * parts_x, parts_x)
    turned = lambda table: np.swapaxes(table, 1, 2)
    rows_in = np.concatenate([turned(high_y), turned(low_y)], axis=1)
    columns_in = np.concatenate([turned(high_x), turned(low_x)], axis=1)
    columns_in = np.concatenate([columns_in, columns_in], axis=2)
    rows_out = np.concatenate([high_y, high_y, low_y], axis=2)
    columns_out = np.concatenate([turned(high_x), turned(low_x)], axis=2)

    other, along_own, squares_own, columns_kept, *kept = analysis(
        model_field,
        driver_field,
        nudge_rate,
        increment_cap,
        rows_in,
        columns_in,
        rows_out,
        columns_out,
    )
    model_kept, rate_rows, cap_rows, rows_out_kept, columns_out_kept = kept
    arriving = lax.ppermute(other, "c", swap)
    mine = contract(along_own, squares_own, columns_kept)

    def exchanged(value):
        blocks = value.reshape(chips, 1, -1)
        return lax.all_to_all(blocks, CHIP, 0, 0, tiled=True).reshape(value.shape)

    own = exchanged(share(exchanged(mine + arriving), chips))
    sibling = lax.ppermute(own, "c", swap)
    cells = float(height * parts_y * width * parts_x)
    limits = rate_rows, cap_rows
    stacks = begin(own, *limits, columns_out_kept, cells)
    return synthesis(
        stacks, sibling, *limits, model_kept, rows_out_kept, columns_out_kept, cells
    )


def solution(mesh):
    finer = Mesh(mesh.devices.reshape(4, 2, 4, 4), ("x", "c", "z", "y"))
    field = P(None, ("x", "c"), ("z", "y"))
    return jax.shard_map(
        per_device,
        mesh=finer,
        in_specs=(field, field, P(), P()),
        out_specs=field,
        check_vma=False,
    )
```

```python
import numpy as np

import jax
import jax.numpy as jnp
import ml_dtypes
from jax import lax
from jax.experimental import pallas as pl
from jax.experimental.pallas import tpu as pltpu
from jax.sharding import Mesh
from jax.sharding import PartitionSpec as P

MODES = 24
WAVES = 2 * MODES
GROUP = 10
TILES = 4
LANES = 128
AHEAD = 3
CHUNK = 10
SLOTS = 16
CHIP = ("x", "z", "y")
EPSILON = 1e-06


def basis_table(length):
    positions = np.arange(length)
    wavenumber = np.concatenate([np.arange(MODES), np.arange(MODES) + 1])
    phases = positions[:, None] * wavenumber[None, :] % length
    angles = phases * (2.0 * np.pi / length)
    column = np.arange(WAVES)
    weights = np.where(column == 0, np.sqrt(1.0 / length), np.sqrt(2.0 / length))
    return np.where(column[None, :] < MODES, np.cos(angles), np.sin(angles)) * weights[None, :]


def split_table(length, parts):
    table = basis_table(length).astype(np.float32)
    high = table.astype(ml_dtypes.bfloat16)
    low = (table - high.astype(np.float32)).astype(ml_dtypes.bfloat16)
    shape = (parts, length // parts, WAVES)
    return high.reshape(shape), low.reshape(shape)


def split(value):
    high = value.astype(jnp.bfloat16)
    low = (value - high.astype(jnp.float32)).astype(jnp.bfloat16)
    return high, low


def dot(left, right, contract):
    return lax.dot_general(left, right, (contract, ((), ())), preferred_element_type=jnp.float32)


def first_contraction(difference, rows, lines, sums, i):
    folded = (difference * difference).reshape(-1, 8, LANES)
    sums[i * 8 : i * 8 + 8, :] = jnp.sum(folded, axis=0)
    product = dot(rows[...], jnp.concatenate(split(difference), axis=1), ((1,), (0,)))
    product = product[:WAVES] + product[WAVES:]
    high, low = split(product[:, :LANES] + product[:, LANES:])
    lines[i * WAVES : (i + 1) * WAVES, :LANES] = high
    lines[i * WAVES : (i + 1) * WAVES, LANES:] = low


def clear_spare(lines, sums):
    spare = (TILES * LANES - GROUP * WAVES, 2 * LANES)
    lines[GROUP * WAVES :, :] = jnp.zeros(spare, lines.dtype)
    sums[GROUP * 8 :, :] = jnp.zeros((8 * (SLOTS - GROUP), LANES), jnp.float32)


def second_contraction(columns, along_y, squares, coefficients, step):
    both = dot(columns[...], along_y[...], ((1,), (1,)))
    both = both[:WAVES] + both[WAVES:]
    total = squares[pl.ds(0, SLOTS, stride=8), :]
    for s in range(1, 8):
        total = total + squares[pl.ds(s, SLOTS, stride=8), :]
    total = jnp.sum(total, axis=1, keepdims=True)
    tiles = [both[:, t * LANES : (t + 1) * LANES] for t in range(TILES)]
    lane = lax.broadcasted_iota(jnp.int32, (SLOTS, LANES), 1)
    top = jnp.where(lane == LANES - 1, total, tiles[-1][:SLOTS])
    tiles[-1] = jnp.concatenate([top, tiles[-1][SLOTS:]], axis=0)
    first = step * TILES * WAVES
    for t in range(TILES):
        coefficients[first + t * WAVES : first + (t + 1) * WAVES, :] = tiles[t]


def analysis_kernel(
    model_hbm, driver_hbm, rate_hbm, cap_hbm, rows_hbm, columns_hbm, rows_out_hbm, columns_out_hbm,
    other, along_own, squares_own, driver_last, rows, columns, model, rate_rows, cap_rows,
    rows_out, columns_out, driver, rate, cap, along_y, squares, arrived, ready,
):
    gy, gx, core = lax.axis_index(("x", "c")), lax.axis_index(("z", "y")), lax.axis_index("c")
    groups = model.shape[0] // GROUP
    half = groups // 2
    tables = [
        pltpu.make_async_copy(rows_hbm.at[gy], rows, ready.at[0]),
        pltpu.make_async_copy(columns_hbm.at[gx], columns, ready.at[1]),
    ]
    later = [
        pltpu.make_async_copy(rate_hbm, rate, ready.at[2]),
        pltpu.make_async_copy(cap_hbm, cap, ready.at[3]),
        pltpu.make_async_copy(rows_out_hbm.at[gy], rows_out, ready.at[4]),
        pltpu.make_async_copy(columns_out_hbm.at[gx], columns_out, ready.at[5]),
    ]

    def ordered(step):
        return lax.rem(step + (1 - core) * half, groups)

    def held(step):
        if step < half:
            return along_y.at[step % 2], squares.at[step % 2]
        return along_own.at[step - half], squares_own.at[step - half]

    def fetch(step):
        span = pl.ds(ordered(step) * GROUP, GROUP)
        kept = driver_last if step == groups - 1 else driver.at[pl.ds(step * GROUP, GROUP)]
        return [
            pltpu.make_async_copy(model_hbm.at[span], model.at[span], arrived.at[0, step]),
            pltpu.make_async_copy(driver_hbm.at[span], kept, arrived.at[1, step]),
        ]

    for copy in tables + fetch(0) + later:
        copy.start()
    for step in range(1, AHEAD):
        for copy in fetch(step):
            copy.start()
    for step in [0, 1, *range(half, groups - 1)]:
        clear_spare(*held(step))

    for step in range(groups):
        for copy in (tables if step == 0 else []) + fetch(step):
            copy.wait()
        if step + AHEAD < groups:
            for copy in fetch(step + AHEAD):
                copy.start()
        for i in range(GROUP) if step < groups - 1 else []:
            difference = driver[step * GROUP + i] - model[ordered(step) * GROUP + i]
            first_contraction(difference, rows, *held(step), i)
            if i == 2 and 0 < step <= half:
                second_contraction(columns, *held(step - 1), other, step - 1)
        if step == 1:
            for copy in later:
                copy.wait()
            for field in range(model.shape[0]):
                place = field // GROUP * SLOTS + field % GROUP
                rate_rows[place : place + 1, :] = jnp.full((1, LANES), rate[field])
                cap_rows[place : place + 1, :] = jnp.full((1, LANES), cap[field])


def contract_kernel(
    along_own, squares_own, driver_last, model, rows, columns, mine, along_y, squares
):
    core = lax.axis_index("c")
    groups = model.shape[0] // GROUP
    half = groups // 2
    base = lax.rem(groups - 1 + (1 - core) * half, groups) * GROUP
    clear_spare(along_y, squares)
    for i in range(GROUP):
        first_contraction(driver_last[i] - model[base + i], rows, along_y, squares, i)
        if i % 3 == 2 and i // 3 < half - 1:
            step = i // 3
            second_contraction(columns, along_own.at[step], squares_own.at[step], mine, step)
    second_contraction(columns, along_y, squares, mine, half - 1)


def tiles_of(coefficients, step):
    first = step * TILES * WAVES
    return [coefficients[first + t * WAVES : first + (t + 1) * WAVES, :] for t in range(TILES)]


def strengths(cells, tiles, rate_rows, cap_rows, group):
    limits = pl.ds(pl.multiple_of(group * SLOTS, SLOTS), SLOTS)
    spread = jnp.sqrt(tiles[-1][:SLOTS, LANES - 1 :] / cells + EPSILON)
    return rate_rows[limits, :] * jnp.minimum(1.0, cap_rows[limits, :] / spread)


def synthesized(tiles, columns):
    high, low = split(jnp.concatenate(tiles, axis=1))
    both = dot(high, columns[...], ((0,), (0,))) + dot(low, columns[...], ((0,), (0,)))
    return both[:, :LANES] + both[:, LANES:]


def stacked(lines, strength):
    high, low = split(lines * strength)
    return jnp.concatenate([high, low, high], axis=0)


def nudge_pair(rows, stacks, models):
    pair = dot(rows[...], jnp.concatenate(stacks, axis=1), ((1,), (0,)))
    return [model + pair[:, j * LANES : (j + 1) * LANES] for j, model in enumerate(models)]


def begin_kernel(cells, own, rate_rows, cap_rows, model, rows, columns, stacks, first_nudged):
    groups = own.shape[0] // (TILES * WAVES)
    base = lax.axis_index("c") * groups
    first = []
    for step in range(groups):
        tiles = tiles_of(own, step)
        strength = strengths(cells, tiles, rate_rows, cap_rows, base + step)
        lines = synthesized(tiles, columns)
        for j in range(GROUP):
            stack = stacked(lines[j * WAVES : (j + 1) * WAVES, :], strength[j : j + 1, :])
            if step > 0:
                stacks[(step - 1) * GROUP + j] = stack
                continue
            first.append(stack)
            if j % 2:
                models = [model[base * GROUP + k] for k in (j - 1, j)]
                pair = nudge_pair(rows, first[j - 1 : j + 1], models)
                first_nudged[j - 1], first_nudged[j] = pair


def synthesis_kernel(
    cells, stacks, first_nudged, sibling, rate_rows, cap_rows, model, rows, columns, nudged_hbm,
    nudged, along_x, strength, leaving,
):
    core = lax.axis_index("c")
    groups = model.shape[0] // GROUP
    half = groups // 2

    def ordered(step):
        return lax.rem(step + core * half, groups)

    def chunk_out(step, first, size):
        span = pl.ds(ordered(step) * GROUP + first, size)
        place = leaving.at[step * (GROUP // CHUNK) + first // CHUNK]
        here = first_nudged if step == 0 else nudged.at[step - 1]
        here = here.at[pl.ds(first, size)]
        return pltpu.make_async_copy(here, nudged_hbm.at[span], place)

    def prepare(step):
        tiles = tiles_of(sibling, step - half)
        strength[step % 2] = strengths(cells, tiles, rate_rows, cap_rows, ordered(step))
        along_x[step % 2] = synthesized(tiles, columns)

    def stack_of(step, j):
        if step < half:
            return stacks[(step - 1) * GROUP + j]
        lines = along_x[step % 2, j * WAVES : (j + 1) * WAVES, :]
        return stacked(lines, strength[step % 2, j : j + 1, :])

    for first in range(0, GROUP, CHUNK):
        chunk_out(0, first, CHUNK).start()
    for step in range(1, groups):
        for i in range(0, GROUP, 2):
            pair = [stack_of(step, j) for j in (i, i + 1)]
            models = [model[ordered(step) * GROUP + j] for j in (i, i + 1)]
            nudged[step - 1, i], nudged[step - 1, i + 1] = nudge_pair(rows, pair, models)
            if i == 0 and half <= step + 1 < groups:
                prepare(step + 1)
            if (i + 2) % CHUNK == 0:
                chunk_out(step, i + 2 - CHUNK, CHUNK).start()
    for step in range(groups):
        for first in range(0, GROUP, CHUNK):
            chunk_out(step, first, CHUNK).wait()


IN_HBM = pl.BlockSpec(memory_space=pltpu.HBM)
IN_VMEM = pl.BlockSpec(memory_space=pltpu.VMEM)
IN_SMEM = pl.BlockSpec(memory_space=pltpu.SMEM)


def share_kernel(chips, pieces, copies, rows):
    height = pieces.shape[0] // chips
    period = 8 * height
    total = pieces[:period, :]
    for first in range(period, pieces.shape[0], period):
        total = total + pieces[first : first + period, :]
    rows[...] = total
    for i in range(height):
        every = pl.ds(i, 8, stride=height)
        line = jnp.sum(rows[every, :], axis=0, keepdims=True)
        rows[every, :] = jnp.broadcast_to(line, (8, LANES))
    for first in range(0, pieces.shape[0], period):
        copies[first : first + period, :] = rows[...]


def share(pieces, chips):
    return pl.pallas_call(
        lambda *refs: share_kernel(chips, *refs),
        out_shape=pltpu.VMEM(pieces.shape, jnp.float32),
        in_specs=[IN_VMEM],
        out_specs=IN_VMEM,
        scratch_shapes=[pltpu.VMEM((8 * pieces.shape[0] // chips, LANES), jnp.float32)],
        compiler_params=pltpu.CompilerParams(vmem_limit_bytes=2 << 20),
        name="share",
    )(kept_in_vmem(pieces))


def kept_in_hbm(value):
    return pltpu.with_memory_space_constraint(value, pltpu.HBM)


def kept_in_vmem(value):
    return pltpu.with_memory_space_constraint(value, pltpu.VMEM)


def analysis(model, driver, rate, cap, rows, columns, rows_out, columns_out):
    groups = model.shape[0] // GROUP
    half = groups // 2
    lines = (TILES * LANES, 2 * LANES)
    sums = (8 * SLOTS, LANES)
    return pl.pallas_call(
        analysis_kernel,
        out_shape=[
            pltpu.VMEM((half * TILES * WAVES, LANES), jnp.float32),
            pltpu.VMEM((half - 1, *lines), jnp.bfloat16),
            pltpu.VMEM((half - 1, *sums), jnp.float32),
            pltpu.VMEM((GROUP, *model.shape[1:]), jnp.float32),
            pltpu.VMEM(rows.shape[1:], jnp.bfloat16),
            pltpu.VMEM(columns.shape[1:], jnp.bfloat16),
            pltpu.VMEM(model.shape, jnp.float32),
            pltpu.VMEM((groups * SLOTS, LANES), jnp.float32),
            pltpu.VMEM((groups * SLOTS, LANES), jnp.float32),
            pltpu.VMEM(rows_out.shape[1:], jnp.bfloat16),
            pltpu.VMEM(columns_out.shape[1:], jnp.bfloat16),
        ],
        in_specs=[IN_HBM] * 8,
        out_specs=[IN_VMEM] * 11,
        scratch_shapes=[
            pltpu.VMEM((model.shape[0] - GROUP, *model.shape[1:]), jnp.float32),
            pltpu.SMEM(rate.shape, jnp.float32),
            pltpu.SMEM(cap.shape, jnp.float32),
            pltpu.VMEM((2, *lines), jnp.bfloat16),
            pltpu.VMEM((2, *sums), jnp.float32),
            pltpu.SemaphoreType.DMA((2, groups)),
            pltpu.SemaphoreType.DMA((6,)),
        ],
        compiler_params=pltpu.CompilerParams(vmem_limit_bytes=16 << 20),
        cost_estimate=estimate(2 * model.size),
        name="analysis",
    )(*map(kept_in_hbm, (model, driver, rate, cap, rows, columns, rows_out, columns_out)))


def contract(along_own, squares_own, driver_last, model, rows, columns):
    half = along_own.shape[0] + 1
    return pl.pallas_call(
        contract_kernel,
        out_shape=pltpu.VMEM((half * TILES * WAVES, LANES), jnp.float32),
        in_specs=[IN_VMEM] * 6,
        out_specs=IN_VMEM,
        scratch_shapes=[
            pltpu.VMEM(along_own.shape[1:], jnp.bfloat16),
            pltpu.VMEM(squares_own.shape[1:], jnp.float32),
        ],
        compiler_params=pltpu.CompilerParams(vmem_limit_bytes=4 << 20),
        cost_estimate=estimate(2 * driver_last.size),
        name="contract",
    )(*map(kept_in_vmem, (along_own, squares_own, driver_last, model, rows, columns)))


def begin(own, rate_rows, cap_rows, model, rows, columns, cells):
    fields = own.shape[0] // (TILES * WAVES) * GROUP - GROUP
    return pl.pallas_call(
        lambda *refs: begin_kernel(cells, *refs),
        out_shape=[
            pltpu.VMEM((fields, 3 * WAVES, LANES), jnp.bfloat16),
            pltpu.VMEM((GROUP, *model.shape[1:]), jnp.float32),
        ],
        in_specs=[IN_VMEM] * 6,
        out_specs=[IN_VMEM] * 2,
        compiler_params=pltpu.CompilerParams(vmem_limit_bytes=4 << 20),
        cost_estimate=estimate(fields * 3 * WAVES * LANES),
        name="begin",
    )(*map(kept_in_vmem, (own, rate_rows, cap_rows, model, rows, columns)))


def synthesis(stacks, first_nudged, sibling, rate_rows, cap_rows, model, rows, columns, cells):
    groups = model.shape[0] // GROUP
    values = stacks, first_nudged, sibling, rate_rows, cap_rows, model, rows, columns
    return pl.pallas_call(
        lambda *refs: synthesis_kernel(cells, *refs),
        out_shape=pltpu.HBM(model.shape, jnp.float32),
        in_specs=[IN_VMEM] * 8,
        out_specs=IN_HBM,
        scratch_shapes=[
            pltpu.VMEM((groups - 1, GROUP, *model.shape[1:]), jnp.float32),
            pltpu.VMEM((2, TILES * LANES, LANES), jnp.float32),
            pltpu.VMEM((2, SLOTS, LANES), jnp.float32),
            pltpu.SemaphoreType.DMA((groups * (GROUP // CHUNK),)),
        ],
        compiler_params=pltpu.CompilerParams(vmem_limit_bytes=12 << 20),
        cost_estimate=estimate(2 * model.size),
        name="synthesis",
    )(*map(kept_in_vmem, values))


def estimate(values):
    return pl.CostEstimate(flops=600 * values, bytes_accessed=4 * values, transcendentals=0)


def per_device(model_field, driver_field, nudge_rate, increment_cap):
    fields, height, width = model_field.shape
    parts_y = lax.axis_size(("x", "c"))
    parts_x = lax.axis_size(("z", "y"))
    chips = lax.axis_size(CHIP)
    swap = [(0, 1), (1, 0)]

    high_y, low_y = split_table(height * parts_y, parts_y)
    high_x, low_x = split_table(width * parts_x, parts_x)
    turned = lambda table: np.swapaxes(table, 1, 2)
    rows_in = np.concatenate([turned(high_y), turned(low_y)], axis=1)
    columns_in = np.concatenate([turned(high_x), turned(low_x)], axis=1)
    columns_in = np.concatenate([columns_in, columns_in], axis=2)
    rows_out = np.concatenate([high_y, high_y, low_y], axis=2)
    columns_out = np.concatenate([turned(high_x), turned(low_x)], axis=2)

    other, along_own, squares_own, driver_last, rows_kept, columns_kept, *kept = analysis(
        model_field,
        driver_field,
        nudge_rate,
        increment_cap,
        rows_in,
        columns_in,
        rows_out,
        columns_out,
    )
    model_kept, rate_rows, cap_rows, rows_out_kept, columns_out_kept = kept
    arriving = lax.ppermute(other, "c", swap)
    mine = contract(along_own, squares_own, driver_last, model_kept, rows_kept, columns_kept)

    def exchanged(value):
        blocks = value.reshape(chips, 1, -1)
        return lax.all_to_all(blocks, CHIP, 0, 0, tiled=True).reshape(value.shape)

    own = exchanged(share(exchanged(mine + arriving), chips))
    sibling = lax.ppermute(own, "c", swap)
    cells = float(height * parts_y * width * parts_x)
    limits = rate_rows, cap_rows
    rest = model_kept, rows_out_kept, columns_out_kept, cells
    stacks, first_nudged = begin(own, *limits, *rest)
    return synthesis(stacks, first_nudged, sibling, *limits, *rest)


def solution(mesh):
    finer = Mesh(mesh.devices.reshape(4, 2, 4, 4), ("x", "c", "z", "y"))
    field = P(None, ("x", "c"), ("z", "y"))
    return jax.shard_map(
        per_device,
        mesh=finer,
        in_specs=(field, field, P(), P()),
        out_specs=field,
        check_vma=False,
    )
```

```python
import numpy as np

import jax
import jax.numpy as jnp
import ml_dtypes
from jax import lax
from jax.experimental import pallas as pl
from jax.experimental.pallas import tpu as pltpu
from jax.sharding import Mesh
from jax.sharding import PartitionSpec as P

MODES = 24
WAVES = 2 * MODES
GROUP = 10
TILES = 4
LANES = 128
AHEAD = 3
TAIL = 4
CHUNK = 10
SLOTS = 16
CHIP = ("x", "z", "y")
EPSILON = 1e-06


def basis_table(length):
    positions = np.arange(length)
    wavenumber = np.concatenate([np.arange(MODES), np.arange(MODES) + 1])
    phases = positions[:, None] * wavenumber[None, :] % length
    angles = phases * (2.0 * np.pi / length)
    column = np.arange(WAVES)
    weights = np.where(column == 0, np.sqrt(1.0 / length), np.sqrt(2.0 / length))
    return np.where(column[None, :] < MODES, np.cos(angles), np.sin(angles)) * weights[None, :]


def split_table(length, parts):
    table = basis_table(length).astype(np.float32)
    high = table.astype(ml_dtypes.bfloat16)
    low = (table - high.astype(np.float32)).astype(ml_dtypes.bfloat16)
    shape = (parts, length // parts, WAVES)
    return high.reshape(shape), low.reshape(shape)


def split(value):
    high = value.astype(jnp.bfloat16)
    low = (value - high.astype(jnp.float32)).astype(jnp.bfloat16)
    return high, low


def dot(left, right, contract):
    return lax.dot_general(left, right, (contract, ((), ())), preferred_element_type=jnp.float32)


def first_contraction(difference, rows, lines, sums, i):
    folded = (difference * difference).reshape(-1, 8, LANES)
    sums[i * 8 : i * 8 + 8, :] = jnp.sum(folded, axis=0)
    product = dot(rows[...], jnp.concatenate(split(difference), axis=1), ((1,), (0,)))
    product = product[:WAVES] + product[WAVES:]
    high, low = split(product[:, :LANES] + product[:, LANES:])
    lines[i * WAVES : (i + 1) * WAVES, :LANES] = high
    lines[i * WAVES : (i + 1) * WAVES, LANES:] = low


def clear_spare(lines, sums):
    spare = (TILES * LANES - GROUP * WAVES, 2 * LANES)
    lines[GROUP * WAVES :, :] = jnp.zeros(spare, lines.dtype)
    sums[GROUP * 8 :, :] = jnp.zeros((8 * (SLOTS - GROUP), LANES), jnp.float32)


def second_contraction(columns, along_y, squares, coefficients, step):
    both = dot(columns[...], along_y[...], ((1,), (1,)))
    both = both[:WAVES] + both[WAVES:]
    total = squares[pl.ds(0, SLOTS, stride=8), :]
    for s in range(1, 8):
        total = total + squares[pl.ds(s, SLOTS, stride=8), :]
    total = jnp.sum(total, axis=1, keepdims=True)
    tiles = [both[:, t * LANES : (t + 1) * LANES] for t in range(TILES)]
    lane = lax.broadcasted_iota(jnp.int32, (SLOTS, LANES), 1)
    top = jnp.where(lane == LANES - 1, total, tiles[-1][:SLOTS])
    tiles[-1] = jnp.concatenate([top, tiles[-1][SLOTS:]], axis=0)
    first = step * TILES * WAVES
    for t in range(TILES):
        coefficients[first + t * WAVES : first + (t + 1) * WAVES, :] = tiles[t]


def analysis_kernel(
    model_hbm, driver_hbm, rate_hbm, cap_hbm, rows_hbm, columns_hbm, rows_out_hbm, columns_out_hbm,
    other, along_own, squares_own, driver_last, rows, columns, model, rate_rows, cap_rows,
    rows_out, columns_out, driver, rate, cap, along_y, squares, arrived, ready,
):
    gy, gx, core = lax.axis_index(("x", "c")), lax.axis_index(("z", "y")), lax.axis_index("c")
    groups = model.shape[0] // GROUP
    half = groups // 2
    tables = [
        pltpu.make_async_copy(rows_hbm.at[gy], rows, ready.at[0]),
        pltpu.make_async_copy(columns_hbm.at[gx], columns, ready.at[1]),
    ]
    later = [
        pltpu.make_async_copy(rate_hbm, rate, ready.at[2]),
        pltpu.make_async_copy(cap_hbm, cap, ready.at[3]),
        pltpu.make_async_copy(rows_out_hbm.at[gy], rows_out, ready.at[4]),
        pltpu.make_async_copy(columns_out_hbm.at[gx], columns_out, ready.at[5]),
    ]

    def ordered(step):
        return lax.rem(step + (1 - core) * half, groups)

    def held(step):
        if step < half:
            return along_y.at[step % 2], squares.at[step % 2]
        return along_own.at[step - half], squares_own.at[step - half]

    def fetch(step):
        last = step == groups - 1
        span = pl.ds(ordered(step) * GROUP, GROUP - TAIL if last else GROUP)
        kept = driver_last if last else driver.at[pl.ds(step * GROUP, GROUP)]
        return [
            pltpu.make_async_copy(model_hbm.at[span], model.at[span], arrived.at[0, step]),
            pltpu.make_async_copy(driver_hbm.at[span], kept, arrived.at[1, step]),
        ]

    for copy in tables + fetch(0) + later:
        copy.start()
    for step in range(1, AHEAD):
        for copy in fetch(step):
            copy.start()
    for step in [0, 1, *range(half, groups - 1)]:
        clear_spare(*held(step))

    for step in range(groups):
        for copy in (tables if step == 0 else []) + fetch(step):
            copy.wait()
        if step + AHEAD < groups:
            for copy in fetch(step + AHEAD):
                copy.start()
        for i in range(GROUP) if step < groups - 1 else []:
            difference = driver[step * GROUP + i] - model[ordered(step) * GROUP + i]
            first_contraction(difference, rows, *held(step), i)
            if i == 2 and 0 < step <= half:
                second_contraction(columns, *held(step - 1), other, step - 1)
        if step == 1:
            for copy in later:
                copy.wait()
            for field in range(model.shape[0]):
                place = field // GROUP * SLOTS + field % GROUP
                rate_rows[place : place + 1, :] = jnp.full((1, LANES), rate[field])
                cap_rows[place : place + 1, :] = jnp.full((1, LANES), cap[field])


def contract_kernel(
    along_own, squares_own, driver_last, model, rows, columns, model_hbm, driver_hbm,
    mine, model_tail, driver_tail, along_y, squares, arrived,
):
    core = lax.axis_index("c")
    groups = model.shape[0] // GROUP
    half = groups // 2
    base = lax.rem(groups - 1 + (1 - core) * half, groups) * GROUP
    span = pl.ds(base + GROUP - TAIL, TAIL)
    copies = [
        pltpu.make_async_copy(model_hbm.at[span], model_tail, arrived.at[0]),
        pltpu.make_async_copy(driver_hbm.at[span], driver_tail, arrived.at[1]),
    ]
    for copy in copies:
        copy.start()
    clear_spare(along_y, squares)
    for i in range(GROUP - TAIL):
        first_contraction(driver_last[i] - model[base + i], rows, along_y, squares, i)
        if i % 2 and i // 2 < half - 1:
            step = i // 2
            second_contraction(columns, along_own.at[step], squares_own.at[step], mine, step)
    for copy in copies:
        copy.wait()
    for i in range(TAIL):
        difference = driver_tail[i] - model_tail[i]
        first_contraction(difference, rows, along_y, squares, GROUP - TAIL + i)
    second_contraction(columns, along_y, squares, mine, half - 1)


def tiles_of(coefficients, step):
    first = step * TILES * WAVES
    return [coefficients[first + t * WAVES : first + (t + 1) * WAVES, :] for t in range(TILES)]


def strengths(cells, tiles, rate_rows, cap_rows, group):
    limits = pl.ds(pl.multiple_of(group * SLOTS, SLOTS), SLOTS)
    spread = jnp.sqrt(tiles[-1][:SLOTS, LANES - 1 :] / cells + EPSILON)
    return rate_rows[limits, :] * jnp.minimum(1.0, cap_rows[limits, :] / spread)


def synthesized(tiles, columns):
    high, low = split(jnp.concatenate(tiles, axis=1))
    both = dot(high, columns[...], ((0,), (0,))) + dot(low, columns[...], ((0,), (0,)))
    return both[:, :LANES] + both[:, LANES:]


def stacked(lines, strength):
    high, low = split(lines * strength)
    return jnp.concatenate([high, low, high], axis=0)


def nudge_pair(rows, stacks, models):
    pair = dot(rows[...], jnp.concatenate(stacks, axis=1), ((1,), (0,)))
    return [model + pair[:, j * LANES : (j + 1) * LANES] for j, model in enumerate(models)]


def begin_kernel(
    cells, own, rate_rows, cap_rows, model, rows, columns, stacks, second, nudged_hbm,
    first, leaving,
):
    groups = own.shape[0] // (TILES * WAVES)
    base = lax.axis_index("c") * groups

    def pair_out(pair):
        here = first.at[pl.ds(2 * pair, 2)]
        there = nudged_hbm.at[pl.ds(base * GROUP + 2 * pair, 2)]
        return pltpu.make_async_copy(here, there, leaving.at[pair])

    for step in range(groups):
        tiles = tiles_of(own, step)
        strength = strengths(cells, tiles, rate_rows, cap_rows, base + step)
        lines = synthesized(tiles, columns)
        for i in range(0, GROUP, 2):
            pair = [
                stacked(lines[j * WAVES : (j + 1) * WAVES, :], strength[j : j + 1, :])
                for j in (i, i + 1)
            ]
            if step == 2:
                stacks[i], stacks[i + 1] = pair
                continue
            models = [model[(base + step) * GROUP + j] for j in (i, i + 1)]
            nudged = first if step == 0 else second
            nudged[i], nudged[i + 1] = nudge_pair(rows, pair, models)
            if step == 0:
                pair_out(i // 2).start()
    for pair in range(GROUP // 2):
        pair_out(pair).wait()


def synthesis_kernel(
    cells, stacks, second, sibling, rate_rows, cap_rows, model, model_tail, rows, columns, begun,
    nudged_hbm, nudged, along_x, strength, leaving,
):
    core = lax.axis_index("c")
    groups = model.shape[0] // GROUP
    half = groups // 2

    def ordered(step):
        return lax.rem(step + core * half, groups)

    def chunk_out(step, first, size):
        span = pl.ds(ordered(step) * GROUP + first, size)
        place = leaving.at[(step - 1) * (GROUP // CHUNK) + first // CHUNK]
        here = second if step == 1 else nudged.at[step - 2]
        here = here.at[pl.ds(first, size)]
        return pltpu.make_async_copy(here, nudged_hbm.at[span], place)

    def prepare(step):
        tiles = tiles_of(sibling, step - half)
        strength[step % 2] = strengths(cells, tiles, rate_rows, cap_rows, ordered(step))
        along_x[step % 2] = synthesized(tiles, columns)

    def stack_of(step, j):
        if step == 2:
            return stacks[j]
        lines = along_x[step % 2, j * WAVES : (j + 1) * WAVES, :]
        return stacked(lines, strength[step % 2, j : j + 1, :])

    def model_of(step, j):
        if step == half - 1 and j >= GROUP - TAIL:
            return model_tail[j - GROUP + TAIL]
        return model[ordered(step) * GROUP + j]

    for first in range(0, GROUP, CHUNK):
        chunk_out(1, first, CHUNK).start()
    for step in range(2, groups):
        for i in range(0, GROUP, 2):
            pair = [stack_of(step, j) for j in (i, i + 1)]
            models = [model_of(step, j) for j in (i, i + 1)]
            nudged[step - 2, i], nudged[step - 2, i + 1] = nudge_pair(rows, pair, models)
            if i == 0 and step + 1 < groups:
                prepare(step + 1)
            if (i + 2) % CHUNK == 0:
                chunk_out(step, i + 2 - CHUNK, CHUNK).start()
    for step in range(1, groups):
        for first in range(0, GROUP, CHUNK):
            chunk_out(step, first, CHUNK).wait()


IN_HBM = pl.BlockSpec(memory_space=pltpu.HBM)
IN_VMEM = pl.BlockSpec(memory_space=pltpu.VMEM)
IN_SMEM = pl.BlockSpec(memory_space=pltpu.SMEM)


def share_kernel(chips, pieces, copies, rows):
    height = pieces.shape[0] // chips
    period = 8 * height
    total = pieces[:period, :]
    for first in range(period, pieces.shape[0], period):
        total = total + pieces[first : first + period, :]
    rows[...] = total
    for i in range(height):
        every = pl.ds(i, 8, stride=height)
        line = jnp.sum(rows[every, :], axis=0, keepdims=True)
        rows[every, :] = jnp.broadcast_to(line, (8, LANES))
    for first in range(0, pieces.shape[0], period):
        copies[first : first + period, :] = rows[...]


def share(pieces, chips):
    return pl.pallas_call(
        lambda *refs: share_kernel(chips, *refs),
        out_shape=pltpu.VMEM(pieces.shape, jnp.float32),
        in_specs=[IN_VMEM],
        out_specs=IN_VMEM,
        scratch_shapes=[pltpu.VMEM((8 * pieces.shape[0] // chips, LANES), jnp.float32)],
        compiler_params=pltpu.CompilerParams(vmem_limit_bytes=2 << 20),
        name="share",
    )(kept_in_vmem(pieces))


def kept_in_hbm(value):
    return pltpu.with_memory_space_constraint(value, pltpu.HBM)


def kept_in_vmem(value):
    return pltpu.with_memory_space_constraint(value, pltpu.VMEM)


def analysis(model, driver, rate, cap, rows, columns, rows_out, columns_out):
    groups = model.shape[0] // GROUP
    half = groups // 2
    lines = (TILES * LANES, 2 * LANES)
    sums = (8 * SLOTS, LANES)
    return pl.pallas_call(
        analysis_kernel,
        out_shape=[
            pltpu.VMEM((half * TILES * WAVES, LANES), jnp.float32),
            pltpu.VMEM((half - 1, *lines), jnp.bfloat16),
            pltpu.VMEM((half - 1, *sums), jnp.float32),
            pltpu.VMEM((GROUP - TAIL, *model.shape[1:]), jnp.float32),
            pltpu.VMEM(rows.shape[1:], jnp.bfloat16),
            pltpu.VMEM(columns.shape[1:], jnp.bfloat16),
            pltpu.VMEM(model.shape, jnp.float32),
            pltpu.VMEM((groups * SLOTS, LANES), jnp.float32),
            pltpu.VMEM((groups * SLOTS, LANES), jnp.float32),
            pltpu.VMEM(rows_out.shape[1:], jnp.bfloat16),
            pltpu.VMEM(columns_out.shape[1:], jnp.bfloat16),
        ],
        in_specs=[IN_HBM] * 8,
        out_specs=[IN_VMEM] * 11,
        scratch_shapes=[
            pltpu.VMEM((model.shape[0] - GROUP, *model.shape[1:]), jnp.float32),
            pltpu.SMEM(rate.shape, jnp.float32),
            pltpu.SMEM(cap.shape, jnp.float32),
            pltpu.VMEM((2, *lines), jnp.bfloat16),
            pltpu.VMEM((2, *sums), jnp.float32),
            pltpu.SemaphoreType.DMA((2, groups)),
            pltpu.SemaphoreType.DMA((6,)),
        ],
        compiler_params=pltpu.CompilerParams(vmem_limit_bytes=16 << 20),
        cost_estimate=estimate(2 * model.size),
        name="analysis",
    )(*map(kept_in_hbm, (model, driver, rate, cap, rows, columns, rows_out, columns_out)))


def contract(along_own, squares_own, driver_last, model, rows, columns, *fields):
    half = along_own.shape[0] + 1
    tail = (TAIL, *model.shape[1:])
    values = along_own, squares_own, driver_last, model, rows, columns
    return pl.pallas_call(
        contract_kernel,
        out_shape=[
            pltpu.VMEM((half * TILES * WAVES, LANES), jnp.float32),
            pltpu.VMEM(tail, jnp.float32),
        ],
        in_specs=[IN_VMEM] * 6 + [IN_HBM] * 2,
        out_specs=[IN_VMEM] * 2,
        scratch_shapes=[
            pltpu.VMEM(tail, jnp.float32),
            pltpu.VMEM(along_own.shape[1:], jnp.bfloat16),
            pltpu.VMEM(squares_own.shape[1:], jnp.float32),
            pltpu.SemaphoreType.DMA((2,)),
        ],
        compiler_params=pltpu.CompilerParams(vmem_limit_bytes=4 << 20),
        cost_estimate=estimate(2 * driver_last.size),
        name="contract",
    )(*map(kept_in_vmem, values), *map(kept_in_hbm, fields))


def begin(own, rate_rows, cap_rows, model, rows, columns, cells):
    group = (GROUP, *model.shape[1:])
    return pl.pallas_call(
        lambda *refs: begin_kernel(cells, *refs),
        out_shape=[
            pltpu.VMEM((GROUP, 3 * WAVES, LANES), jnp.bfloat16),
            pltpu.VMEM(group, jnp.float32),
            pltpu.HBM(model.shape, jnp.float32),
        ],
        in_specs=[IN_VMEM] * 6,
        out_specs=[IN_VMEM, IN_VMEM, IN_HBM],
        scratch_shapes=[
            pltpu.VMEM(group, jnp.float32),
            pltpu.SemaphoreType.DMA((GROUP // 2,)),
        ],
        compiler_params=pltpu.CompilerParams(vmem_limit_bytes=4 << 20),
        cost_estimate=estimate(2 * GROUP * model.shape[1] * model.shape[2]),
        name="begin",
    )(*map(kept_in_vmem, (own, rate_rows, cap_rows, model, rows, columns)))


def synthesis(begun, stacks, second, sibling, limits, model, model_tail, rows, columns, cells):
    groups = model.shape[0] // GROUP
    values = stacks, second, sibling, *limits, model, model_tail, rows, columns
    return pl.pallas_call(
        lambda *refs: synthesis_kernel(cells, *refs),
        out_shape=pltpu.HBM(model.shape, jnp.float32),
        in_specs=[IN_VMEM] * 9 + [IN_HBM],
        out_specs=IN_HBM,
        input_output_aliases={9: 0},
        scratch_shapes=[
            pltpu.VMEM((groups - 2, GROUP, *model.shape[1:]), jnp.float32),
            pltpu.VMEM((2, TILES * LANES, LANES), jnp.float32),
            pltpu.VMEM((2, SLOTS, LANES), jnp.float32),
            pltpu.SemaphoreType.DMA(((groups - 1) * (GROUP // CHUNK),)),
        ],
        compiler_params=pltpu.CompilerParams(vmem_limit_bytes=12 << 20),
        cost_estimate=estimate(2 * model.size),
        name="synthesis",
    )(*map(kept_in_vmem, values), kept_in_hbm(begun))


def estimate(values):
    return pl.CostEstimate(flops=600 * values, bytes_accessed=4 * values, transcendentals=0)


def per_device(model_field, driver_field, nudge_rate, increment_cap):
    fields, height, width = model_field.shape
    parts_y = lax.axis_size(("x", "c"))
    parts_x = lax.axis_size(("z", "y"))
    chips = lax.axis_size(CHIP)
    swap = [(0, 1), (1, 0)]

    high_y, low_y = split_table(height * parts_y, parts_y)
    high_x, low_x = split_table(width * parts_x, parts_x)
    turned = lambda table: np.swapaxes(table, 1, 2)
    rows_in = np.concatenate([turned(high_y), turned(low_y)], axis=1)
    columns_in = np.concatenate([turned(high_x), turned(low_x)], axis=1)
    columns_in = np.concatenate([columns_in, columns_in], axis=2)
    rows_out = np.concatenate([high_y, high_y, low_y], axis=2)
    columns_out = np.concatenate([turned(high_x), turned(low_x)], axis=2)

    other, along_own, squares_own, driver_last, rows_kept, columns_kept, *kept = analysis(
        model_field,
        driver_field,
        nudge_rate,
        increment_cap,
        rows_in,
        columns_in,
        rows_out,
        columns_out,
    )
    model_kept, rate_rows, cap_rows, rows_out_kept, columns_out_kept = kept
    arriving = lax.ppermute(other, "c", swap)
    own_lines = along_own, squares_own, driver_last
    tables_kept = rows_kept, columns_kept
    mine, model_tail = contract(
        *own_lines, model_kept, *tables_kept, model_field, driver_field
    )

    def exchanged(value):
        blocks = value.reshape(chips, 1, -1)
        return lax.all_to_all(blocks, CHIP, 0, 0, tiled=True).reshape(value.shape)

    own = exchanged(share(exchanged(mine + arriving), chips))
    sibling = lax.ppermute(own, "c", swap)
    cells = float(height * parts_y * width * parts_x)
    limits = rate_rows, cap_rows
    rest = rows_out_kept, columns_out_kept, cells
    stacks, second, begun = begin(own, *limits, model_kept, *rest)
    return synthesis(begun, stacks, second, sibling, limits, model_kept, model_tail, *rest)


def solution(mesh):
    finer = Mesh(mesh.devices.reshape(4, 2, 4, 4), ("x", "c", "z", "y"))
    field = P(None, ("x", "c"), ("z", "y"))
    return jax.shard_map(
        per_device,
        mesh=finer,
        in_specs=(field, field, P(), P()),
        out_specs=field,
        check_vma=False,
    )
```

```python
import numpy as np

import jax
import jax.numpy as jnp
import ml_dtypes
from jax import lax
from jax.experimental import pallas as pl
from jax.experimental.pallas import tpu as pltpu
from jax.sharding import Mesh
from jax.sharding import PartitionSpec as P

MODES = 24
WAVES = 2 * MODES
GROUP = 10
TILES = 4
LANES = 128
AHEAD = 3
TAIL = 3
LAST_CHUNKS = (6, 4)
SLOTS = 16
CHIP = ("x", "z", "y")
EPSILON = 1e-06


def basis_table(length):
    positions = np.arange(length)
    wavenumber = np.concatenate([np.arange(MODES), np.arange(MODES) + 1])
    phases = positions[:, None] * wavenumber[None, :] % length
    angles = phases * (2.0 * np.pi / length)
    column = np.arange(WAVES)
    weights = np.where(column == 0, np.sqrt(1.0 / length), np.sqrt(2.0 / length))
    return np.where(column[None, :] < MODES, np.cos(angles), np.sin(angles)) * weights[None, :]


def split_table(length, parts):
    table = basis_table(length).astype(np.float32)
    high = table.astype(ml_dtypes.bfloat16)
    low = (table - high.astype(np.float32)).astype(ml_dtypes.bfloat16)
    shape = (parts, length // parts, WAVES)
    return high.reshape(shape), low.reshape(shape)


def split(value):
    high = value.astype(jnp.bfloat16)
    low = (value - high.astype(jnp.float32)).astype(jnp.bfloat16)
    return high, low


def dot(left, right, contract):
    return lax.dot_general(left, right, (contract, ((), ())), preferred_element_type=jnp.float32)


def first_contraction(difference, rows, lines, sums, i):
    folded = (difference * difference).reshape(-1, 8, LANES)
    sums[i * 8 : i * 8 + 8, :] = jnp.sum(folded, axis=0)
    product = dot(rows[...], jnp.concatenate(split(difference), axis=1), ((1,), (0,)))
    product = product[:WAVES] + product[WAVES:]
    high, low = split(product[:, :LANES] + product[:, LANES:])
    lines[i * WAVES : (i + 1) * WAVES, :LANES] = high
    lines[i * WAVES : (i + 1) * WAVES, LANES:] = low


def clear_spare(lines, sums):
    spare = (TILES * LANES - GROUP * WAVES, 2 * LANES)
    lines[GROUP * WAVES :, :] = jnp.zeros(spare, lines.dtype)
    sums[GROUP * 8 :, :] = jnp.zeros((8 * (SLOTS - GROUP), LANES), jnp.float32)


def second_contraction(columns, along_y, squares, coefficients, step):
    both = dot(columns[...], along_y[...], ((1,), (1,)))
    both = both[:WAVES] + both[WAVES:]
    total = squares[pl.ds(0, SLOTS, stride=8), :]
    for s in range(1, 8):
        total = total + squares[pl.ds(s, SLOTS, stride=8), :]
    total = jnp.sum(total, axis=1, keepdims=True)
    tiles = [both[:, t * LANES : (t + 1) * LANES] for t in range(TILES)]
    lane = lax.broadcasted_iota(jnp.int32, (SLOTS, LANES), 1)
    top = jnp.where(lane == LANES - 1, total, tiles[-1][:SLOTS])
    tiles[-1] = jnp.concatenate([top, tiles[-1][SLOTS:]], axis=0)
    first = step * TILES * WAVES
    for t in range(TILES):
        coefficients[first + t * WAVES : first + (t + 1) * WAVES, :] = tiles[t]


def analysis_kernel(
    model_hbm, driver_hbm, rate_hbm, cap_hbm, rows_hbm, columns_hbm, rows_out_hbm, columns_out_hbm,
    other, along_own, squares_own, driver_last, rows, columns, model, rate_rows, cap_rows,
    rows_out, columns_out, driver, rate, cap, along_y, squares, arrived, ready,
):
    gy, gx, core = lax.axis_index(("x", "c")), lax.axis_index(("z", "y")), lax.axis_index("c")
    groups = model.shape[0] // GROUP
    half = groups // 2
    tables = [
        pltpu.make_async_copy(rows_hbm.at[gy], rows, ready.at[0]),
        pltpu.make_async_copy(columns_hbm.at[gx], columns, ready.at[1]),
    ]
    later = [
        pltpu.make_async_copy(rate_hbm, rate, ready.at[2]),
        pltpu.make_async_copy(cap_hbm, cap, ready.at[3]),
        pltpu.make_async_copy(rows_out_hbm.at[gy], rows_out, ready.at[4]),
        pltpu.make_async_copy(columns_out_hbm.at[gx], columns_out, ready.at[5]),
    ]

    def ordered(step):
        return lax.rem(step + (1 - core) * half, groups)

    def held(step):
        if step < half:
            return along_y.at[step % 2], squares.at[step % 2]
        return along_own.at[step - half], squares_own.at[step - half]

    def fetch(step):
        last = step == groups - 1
        span = pl.ds(ordered(step) * GROUP, GROUP - TAIL if last else GROUP)
        kept = driver_last if last else driver.at[pl.ds(step * GROUP, GROUP)]
        return [
            pltpu.make_async_copy(model_hbm.at[span], model.at[span], arrived.at[0, step]),
            pltpu.make_async_copy(driver_hbm.at[span], kept, arrived.at[1, step]),
        ]

    for copy in tables + fetch(0) + later:
        copy.start()
    for step in range(1, AHEAD):
        for copy in fetch(step):
            copy.start()
    for step in [0, 1, *range(half, groups - 1)]:
        clear_spare(*held(step))

    for step in range(groups):
        for copy in (tables if step == 0 else []) + fetch(step):
            copy.wait()
        if step + AHEAD < groups:
            for copy in fetch(step + AHEAD):
                copy.start()
        for i in range(GROUP) if step < groups - 1 else []:
            difference = driver[step * GROUP + i] - model[ordered(step) * GROUP + i]
            first_contraction(difference, rows, *held(step), i)
            if i == 2 and 0 < step <= half:
                second_contraction(columns, *held(step - 1), other, step - 1)
        if step == 1:
            for copy in later:
                copy.wait()
            for field in range(model.shape[0]):
                place = field // GROUP * SLOTS + field % GROUP
                rate_rows[place : place + 1, :] = jnp.full((1, LANES), rate[field])
                cap_rows[place : place + 1, :] = jnp.full((1, LANES), cap[field])


def contract_kernel(
    along_own, squares_own, driver_last, model, rows, columns, model_hbm, driver_hbm,
    mine, model_tail, driver_tail, along_y, squares, arrived,
):
    core = lax.axis_index("c")
    groups = model.shape[0] // GROUP
    half = groups // 2
    base = lax.rem(groups - 1 + (1 - core) * half, groups) * GROUP
    span = pl.ds(base + GROUP - TAIL, TAIL)
    copies = [
        pltpu.make_async_copy(model_hbm.at[span], model_tail, arrived.at[0]),
        pltpu.make_async_copy(driver_hbm.at[span], driver_tail, arrived.at[1]),
    ]
    for copy in copies:
        copy.start()
    clear_spare(along_y, squares)
    for i in range(GROUP - TAIL):
        first_contraction(driver_last[i] - model[base + i], rows, along_y, squares, i)
        if i % 2 and i // 2 < half - 1:
            step = i // 2
            second_contraction(columns, along_own.at[step], squares_own.at[step], mine, step)
    for copy in copies:
        copy.wait()
    for i in range(TAIL):
        difference = driver_tail[i] - model_tail[i]
        first_contraction(difference, rows, along_y, squares, GROUP - TAIL + i)
    second_contraction(columns, along_y, squares, mine, half - 1)


def tiles_of(coefficients, step):
    first = step * TILES * WAVES
    return [coefficients[first + t * WAVES : first + (t + 1) * WAVES, :] for t in range(TILES)]


def strengths(cells, tiles, rate_rows, cap_rows, group):
    limits = pl.ds(pl.multiple_of(group * SLOTS, SLOTS), SLOTS)
    spread = jnp.sqrt(tiles[-1][:SLOTS, LANES - 1 :] / cells + EPSILON)
    return rate_rows[limits, :] * jnp.minimum(1.0, cap_rows[limits, :] / spread)


def synthesized(tiles, columns):
    high, low = split(jnp.concatenate(tiles, axis=1))
    both = dot(high, columns[...], ((0,), (0,))) + dot(low, columns[...], ((0,), (0,)))
    return both[:, :LANES] + both[:, LANES:]


def stacked(lines, strength):
    high, low = split(lines * strength)
    return jnp.concatenate([high, low, high], axis=0)


def nudge_pair(rows, stacks, models):
    pair = dot(rows[...], jnp.concatenate(stacks, axis=1), ((1,), (0,)))
    return [model + pair[:, j * LANES : (j + 1) * LANES] for j, model in enumerate(models)]


def begin_kernel(
    cells, own, rate_rows, cap_rows, model, rows, columns, stacks, second, nudged_hbm,
    first, leaving,
):
    groups = own.shape[0] // (TILES * WAVES)
    base = lax.axis_index("c") * groups

    def pair_out(pair):
        here = first.at[pl.ds(2 * pair, 2)]
        there = nudged_hbm.at[pl.ds(base * GROUP + 2 * pair, 2)]
        return pltpu.make_async_copy(here, there, leaving.at[pair])

    for step in range(groups):
        tiles = tiles_of(own, step)
        strength = strengths(cells, tiles, rate_rows, cap_rows, base + step)
        lines = synthesized(tiles, columns)
        for i in range(0, GROUP, 2):
            pair = [
                stacked(lines[j * WAVES : (j + 1) * WAVES, :], strength[j : j + 1, :])
                for j in (i, i + 1)
            ]
            if step == 2:
                stacks[i], stacks[i + 1] = pair
                continue
            models = [model[(base + step) * GROUP + j] for j in (i, i + 1)]
            nudged = first if step == 0 else second
            nudged[i], nudged[i + 1] = nudge_pair(rows, pair, models)
            if step == 0:
                pair_out(i // 2).start()
    for pair in range(GROUP // 2):
        pair_out(pair).wait()


def synthesis_kernel(
    cells, stacks, second, sibling, rate_rows, cap_rows, model, model_tail, rows, columns, begun,
    nudged_hbm, nudged, along_x, strength, leaving,
):
    core = lax.axis_index("c")
    groups = model.shape[0] // GROUP
    half = groups // 2

    def ordered(step):
        return lax.rem(step + core * half, groups)

    chunks = {}
    for step in range(1, groups):
        first = 0
        for size in LAST_CHUNKS if step == groups - 1 else (GROUP,):
            chunks[step, first + size] = first, size, len(chunks)
            first += size

    def chunk_out(step, end):
        first, size, place = chunks[step, end]
        span = pl.ds(ordered(step) * GROUP + first, size)
        here = second if step == 1 else nudged.at[step - 2]
        here = here.at[pl.ds(first, size)]
        return pltpu.make_async_copy(here, nudged_hbm.at[span], leaving.at[place])

    def prepare(step):
        tiles = tiles_of(sibling, step - half)
        strength[step % 2] = strengths(cells, tiles, rate_rows, cap_rows, ordered(step))
        along_x[step % 2] = synthesized(tiles, columns)

    def stack_of(step, j):
        if step == 2:
            return stacks[j]
        lines = along_x[step % 2, j * WAVES : (j + 1) * WAVES, :]
        return stacked(lines, strength[step % 2, j : j + 1, :])

    def model_of(step, j):
        if step == half - 1 and j >= GROUP - TAIL:
            return model_tail[j - GROUP + TAIL]
        return model[ordered(step) * GROUP + j]

    chunk_out(1, GROUP).start()
    for step in range(2, groups):
        for i in range(0, GROUP, 2):
            pair = [stack_of(step, j) for j in (i, i + 1)]
            models = [model_of(step, j) for j in (i, i + 1)]
            nudged[step - 2, i], nudged[step - 2, i + 1] = nudge_pair(rows, pair, models)
            if i == 0 and step + 1 < groups:
                prepare(step + 1)
            if (step, i + 2) in chunks:
                chunk_out(step, i + 2).start()
    for step, end in chunks:
        chunk_out(step, end).wait()


IN_HBM = pl.BlockSpec(memory_space=pltpu.HBM)
IN_VMEM = pl.BlockSpec(memory_space=pltpu.VMEM)
IN_SMEM = pl.BlockSpec(memory_space=pltpu.SMEM)


def share_kernel(chips, pieces, copies, rows):
    height = pieces.shape[0] // chips
    period = 8 * height
    total = pieces[:period, :]
    for first in range(period, pieces.shape[0], period):
        total = total + pieces[first : first + period, :]
    rows[...] = total
    for i in range(height):
        every = pl.ds(i, 8, stride=height)
        line = jnp.sum(rows[every, :], axis=0, keepdims=True)
        rows[every, :] = jnp.broadcast_to(line, (8, LANES))
    for first in range(0, pieces.shape[0], period):
        copies[first : first + period, :] = rows[...]


def share(pieces, chips):
    return pl.pallas_call(
        lambda *refs: share_kernel(chips, *refs),
        out_shape=pltpu.VMEM(pieces.shape, jnp.float32),
        in_specs=[IN_VMEM],
        out_specs=IN_VMEM,
        scratch_shapes=[pltpu.VMEM((8 * pieces.shape[0] // chips, LANES), jnp.float32)],
        compiler_params=pltpu.CompilerParams(vmem_limit_bytes=2 << 20),
        name="share",
    )(kept_in_vmem(pieces))


def kept_in_hbm(value):
    return pltpu.with_memory_space_constraint(value, pltpu.HBM)


def kept_in_vmem(value):
    return pltpu.with_memory_space_constraint(value, pltpu.VMEM)


def analysis(model, driver, rate, cap, rows, columns, rows_out, columns_out):
    groups = model.shape[0] // GROUP
    half = groups // 2
    lines = (TILES * LANES, 2 * LANES)
    sums = (8 * SLOTS, LANES)
    return pl.pallas_call(
        analysis_kernel,
        out_shape=[
            pltpu.VMEM((half * TILES * WAVES, LANES), jnp.float32),
            pltpu.VMEM((half - 1, *lines), jnp.bfloat16),
            pltpu.VMEM((half - 1, *sums), jnp.float32),
            pltpu.VMEM((GROUP - TAIL, *model.shape[1:]), jnp.float32),
            pltpu.VMEM(rows.shape[1:], jnp.bfloat16),
            pltpu.VMEM(columns.shape[1:], jnp.bfloat16),
            pltpu.VMEM(model.shape, jnp.float32),
            pltpu.VMEM((groups * SLOTS, LANES), jnp.float32),
            pltpu.VMEM((groups * SLOTS, LANES), jnp.float32),
            pltpu.VMEM(rows_out.shape[1:], jnp.bfloat16),
            pltpu.VMEM(columns_out.shape[1:], jnp.bfloat16),
        ],
        in_specs=[IN_HBM] * 8,
        out_specs=[IN_VMEM] * 11,
        scratch_shapes=[
            pltpu.VMEM((model.shape[0] - GROUP, *model.shape[1:]), jnp.float32),
            pltpu.SMEM(rate.shape, jnp.float32),
            pltpu.SMEM(cap.shape, jnp.float32),
            pltpu.VMEM((2, *lines), jnp.bfloat16),
            pltpu.VMEM((2, *sums), jnp.float32),
            pltpu.SemaphoreType.DMA((2, groups)),
            pltpu.SemaphoreType.DMA((6,)),
        ],
        compiler_params=pltpu.CompilerParams(vmem_limit_bytes=16 << 20),
        cost_estimate=estimate(2 * model.size),
        name="analysis",
    )(*map(kept_in_hbm, (model, driver, rate, cap, rows, columns, rows_out, columns_out)))


def contract(along_own, squares_own, driver_last, model, rows, columns, *fields):
    half = along_own.shape[0] + 1
    tail = (TAIL, *model.shape[1:])
    values = along_own, squares_own, driver_last, model, rows, columns
    return pl.pallas_call(
        contract_kernel,
        out_shape=[
            pltpu.VMEM((half * TILES * WAVES, LANES), jnp.float32),
            pltpu.VMEM(tail, jnp.float32),
        ],
        in_specs=[IN_VMEM] * 6 + [IN_HBM] * 2,
        out_specs=[IN_VMEM] * 2,
        scratch_shapes=[
            pltpu.VMEM(tail, jnp.float32),
            pltpu.VMEM(along_own.shape[1:], jnp.bfloat16),
            pltpu.VMEM(squares_own.shape[1:], jnp.float32),
            pltpu.SemaphoreType.DMA((2,)),
        ],
        compiler_params=pltpu.CompilerParams(vmem_limit_bytes=4 << 20),
        cost_estimate=estimate(2 * driver_last.size),
        name="contract",
    )(*map(kept_in_vmem, values), *map(kept_in_hbm, fields))


def begin(own, rate_rows, cap_rows, model, rows, columns, cells):
    group = (GROUP, *model.shape[1:])
    return pl.pallas_call(
        lambda *refs: begin_kernel(cells, *refs),
        out_shape=[
            pltpu.VMEM((GROUP, 3 * WAVES, LANES), jnp.bfloat16),
            pltpu.VMEM(group, jnp.float32),
            pltpu.HBM(model.shape, jnp.float32),
        ],
        in_specs=[IN_VMEM] * 6,
        out_specs=[IN_VMEM, IN_VMEM, IN_HBM],
        scratch_shapes=[
            pltpu.VMEM(group, jnp.float32),
            pltpu.SemaphoreType.DMA((GROUP // 2,)),
        ],
        compiler_params=pltpu.CompilerParams(vmem_limit_bytes=4 << 20),
        cost_estimate=estimate(2 * GROUP * model.shape[1] * model.shape[2]),
        name="begin",
    )(*map(kept_in_vmem, (own, rate_rows, cap_rows, model, rows, columns)))


def synthesis(begun, stacks, second, sibling, limits, model, model_tail, rows, columns, cells):
    groups = model.shape[0] // GROUP
    values = stacks, second, sibling, *limits, model, model_tail, rows, columns
    return pl.pallas_call(
        lambda *refs: synthesis_kernel(cells, *refs),
        out_shape=pltpu.HBM(model.shape, jnp.float32),
        in_specs=[IN_VMEM] * 9 + [IN_HBM],
        out_specs=IN_HBM,
        input_output_aliases={9: 0},
        scratch_shapes=[
            pltpu.VMEM((groups - 2, GROUP, *model.shape[1:]), jnp.float32),
            pltpu.VMEM((2, TILES * LANES, LANES), jnp.float32),
            pltpu.VMEM((2, SLOTS, LANES), jnp.float32),
            pltpu.SemaphoreType.DMA((groups - 2 + len(LAST_CHUNKS),)),
        ],
        compiler_params=pltpu.CompilerParams(vmem_limit_bytes=12 << 20),
        cost_estimate=estimate(2 * model.size),
        name="synthesis",
    )(*map(kept_in_vmem, values), kept_in_hbm(begun))


def estimate(values):
    return pl.CostEstimate(flops=600 * values, bytes_accessed=4 * values, transcendentals=0)


def per_device(model_field, driver_field, nudge_rate, increment_cap):
    fields, height, width = model_field.shape
    parts_y = lax.axis_size(("x", "c"))
    parts_x = lax.axis_size(("z", "y"))
    chips = lax.axis_size(CHIP)
    swap = [(0, 1), (1, 0)]

    high_y, low_y = split_table(height * parts_y, parts_y)
    high_x, low_x = split_table(width * parts_x, parts_x)
    turned = lambda table: np.swapaxes(table, 1, 2)
    rows_in = np.concatenate([turned(high_y), turned(low_y)], axis=1)
    columns_in = np.concatenate([turned(high_x), turned(low_x)], axis=1)
    columns_in = np.concatenate([columns_in, columns_in], axis=2)
    rows_out = np.concatenate([high_y, high_y, low_y], axis=2)
    columns_out = np.concatenate([turned(high_x), turned(low_x)], axis=2)

    other, along_own, squares_own, driver_last, rows_kept, columns_kept, *kept = analysis(
        model_field,
        driver_field,
        nudge_rate,
        increment_cap,
        rows_in,
        columns_in,
        rows_out,
        columns_out,
    )
    model_kept, rate_rows, cap_rows, rows_out_kept, columns_out_kept = kept
    arriving = lax.ppermute(other, "c", swap)
    own_lines = along_own, squares_own, driver_last
    tables_kept = rows_kept, columns_kept
    mine, model_tail = contract(
        *own_lines, model_kept, *tables_kept, model_field, driver_field
    )

    def exchanged(value):
        blocks = value.reshape(chips, 1, -1)
        return lax.all_to_all(blocks, CHIP, 0, 0, tiled=True).reshape(value.shape)

    own = exchanged(share(exchanged(mine + arriving), chips))
    sibling = lax.ppermute(own, "c", swap)
    cells = float(height * parts_y * width * parts_x)
    limits = rate_rows, cap_rows
    rest = rows_out_kept, columns_out_kept, cells
    stacks, second, begun = begin(own, *limits, model_kept, *rest)
    return synthesis(begun, stacks, second, sibling, limits, model_kept, model_tail, *rest)


def solution(mesh):
    finer = Mesh(mesh.devices.reshape(4, 2, 4, 4), ("x", "c", "z", "y"))
    field = P(None, ("x", "c"), ("z", "y"))
    return jax.shard_map(
        per_device,
        mesh=finer,
        in_specs=(field, field, P(), P()),
        out_specs=field,
        check_vma=False,
    )
```

```python
import numpy as np

import jax
import jax.numpy as jnp
import ml_dtypes
from jax import lax
from jax.experimental import pallas as pl
from jax.experimental.pallas import tpu as pltpu
from jax.sharding import Mesh
from jax.sharding import PartitionSpec as P

MODES = 24
WAVES = 2 * MODES
GROUP = 10
TILES = 4
LANES = 128
AHEAD = 3
TAIL = 3
CHUNK = 10
SLOTS = 16
CHIP = ("x", "z", "y")
EPSILON = 1e-06


def basis_table(length):
    positions = np.arange(length)
    wavenumber = np.concatenate([np.arange(MODES), np.arange(MODES) + 1])
    phases = positions[:, None] * wavenumber[None, :] % length
    angles = phases * (2.0 * np.pi / length)
    column = np.arange(WAVES)
    weights = np.where(column == 0, np.sqrt(1.0 / length), np.sqrt(2.0 / length))
    return np.where(column[None, :] < MODES, np.cos(angles), np.sin(angles)) * weights[None, :]


def split_table(length, parts):
    table = basis_table(length).astype(np.float32)
    high = table.astype(ml_dtypes.bfloat16)
    low = (table - high.astype(np.float32)).astype(ml_dtypes.bfloat16)
    shape = (parts, length // parts, WAVES)
    return high.reshape(shape), low.reshape(shape)


def split(value):
    high = value.astype(jnp.bfloat16)
    low = (value - high.astype(jnp.float32)).astype(jnp.bfloat16)
    return high, low


def dot(left, right, contract):
    return lax.dot_general(left, right, (contract, ((), ())), preferred_element_type=jnp.float32)


def first_contraction(difference, rows, lines, sums, i):
    folded = (difference * difference).reshape(-1, 8, LANES)
    sums[i * 8 : i * 8 + 8, :] = jnp.sum(folded, axis=0)
    product = dot(rows[...], jnp.concatenate(split(difference), axis=1), ((1,), (0,)))
    product = product[:WAVES] + product[WAVES:]
    high, low = split(product[:, :LANES] + product[:, LANES:])
    lines[i * WAVES : (i + 1) * WAVES, :LANES] = high
    lines[i * WAVES : (i + 1) * WAVES, LANES:] = low


def clear_spare(lines, sums):
    spare = (TILES * LANES - GROUP * WAVES, 2 * LANES)
    lines[GROUP * WAVES :, :] = jnp.zeros(spare, lines.dtype)
    sums[GROUP * 8 :, :] = jnp.zeros((8 * (SLOTS - GROUP), LANES), jnp.float32)


def second_contraction(columns, along_y, squares, coefficients, step):
    both = dot(columns[...], along_y[...], ((1,), (1,)))
    both = both[:WAVES] + both[WAVES:]
    total = squares[pl.ds(0, SLOTS, stride=8), :]
    for s in range(1, 8):
        total = total + squares[pl.ds(s, SLOTS, stride=8), :]
    total = jnp.sum(total, axis=1, keepdims=True)
    tiles = [both[:, t * LANES : (t + 1) * LANES] for t in range(TILES)]
    lane = lax.broadcasted_iota(jnp.int32, (SLOTS, LANES), 1)
    top = jnp.where(lane == LANES - 1, total, tiles[-1][:SLOTS])
    tiles[-1] = jnp.concatenate([top, tiles[-1][SLOTS:]], axis=0)
    first = step * TILES * WAVES
    for t in range(TILES):
        coefficients[first + t * WAVES : first + (t + 1) * WAVES, :] = tiles[t]


def analysis_kernel(
    model_hbm, driver_hbm, rate_hbm, cap_hbm, rows_hbm, columns_hbm, rows_out_hbm, columns_out_hbm,
    other, along_own, squares_own, driver_last, rows, columns, model, rate_rows, cap_rows,
    rows_out, columns_out, driver, rate, cap, along_y, squares, arrived, ready,
):
    gy, gx, core = lax.axis_index(("x", "c")), lax.axis_index(("z", "y")), lax.axis_index("c")
    groups = model.shape[0] // GROUP
    half = groups // 2
    tables = [
        pltpu.make_async_copy(rows_hbm.at[gy], rows, ready.at[0]),
        pltpu.make_async_copy(columns_hbm.at[gx], columns, ready.at[1]),
    ]
    later = [
        pltpu.make_async_copy(rate_hbm, rate, ready.at[2]),
        pltpu.make_async_copy(cap_hbm, cap, ready.at[3]),
        pltpu.make_async_copy(rows_out_hbm.at[gy], rows_out, ready.at[4]),
        pltpu.make_async_copy(columns_out_hbm.at[gx], columns_out, ready.at[5]),
    ]

    def ordered(step):
        return lax.rem(step + (1 - core) * half, groups)

    def held(step):
        if step < half:
            return along_y.at[step % 2], squares.at[step % 2]
        return along_own.at[step - half], squares_own.at[step - half]

    def fetch(step):
        last = step == groups - 1
        span = pl.ds(ordered(step) * GROUP, GROUP - TAIL if last else GROUP)
        kept = driver_last if last else driver.at[pl.ds(step * GROUP, GROUP)]
        return [
            pltpu.make_async_copy(model_hbm.at[span], model.at[span], arrived.at[0, step]),
            pltpu.make_async_copy(driver_hbm.at[span], kept, arrived.at[1, step]),
        ]

    for copy in tables + fetch(0) + later:
        copy.start()
    for step in range(1, AHEAD):
        for copy in fetch(step):
            copy.start()
    for step in [0, 1, *range(half, groups - 1)]:
        clear_spare(*held(step))

    for step in range(groups):
        for copy in (tables if step == 0 else []) + fetch(step):
            copy.wait()
        if step + AHEAD < groups:
            for copy in fetch(step + AHEAD):
                copy.start()
        for i in range(GROUP) if step < groups - 1 else []:
            difference = driver[step * GROUP + i] - model[ordered(step) * GROUP + i]
            first_contraction(difference, rows, *held(step), i)
            if i == 2 and 0 < step <= half:
                second_contraction(columns, *held(step - 1), other, step - 1)
        if step == 1:
            for copy in later:
                copy.wait()
            for field in range(model.shape[0]):
                place = field // GROUP * SLOTS + field % GROUP
                rate_rows[place : place + 1, :] = jnp.full((1, LANES), rate[field])
                cap_rows[place : place + 1, :] = jnp.full((1, LANES), cap[field])


def contract_kernel(
    along_own, squares_own, driver_last, model, rows, columns, model_hbm, driver_hbm,
    mine, model_tail, driver_tail, along_y, squares, arrived,
):
    core = lax.axis_index("c")
    groups = model.shape[0] // GROUP
    half = groups // 2
    base = lax.rem(groups - 1 + (1 - core) * half, groups) * GROUP
    span = pl.ds(base + GROUP - TAIL, TAIL)
    copies = [
        pltpu.make_async_copy(model_hbm.at[span], model_tail, arrived.at[0]),
        pltpu.make_async_copy(driver_hbm.at[span], driver_tail, arrived.at[1]),
    ]
    for copy in copies:
        copy.start()
    clear_spare(along_y, squares)
    for i in range(GROUP - TAIL):
        first_contraction(driver_last[i] - model[base + i], rows, along_y, squares, i)
        if i % 2 and i // 2 < half - 1:
            step = i // 2
            second_contraction(columns, along_own.at[step], squares_own.at[step], mine, step)
    for copy in copies:
        copy.wait()
    for i in range(TAIL):
        difference = driver_tail[i] - model_tail[i]
        first_contraction(difference, rows, along_y, squares, GROUP - TAIL + i)
    second_contraction(columns, along_y, squares, mine, half - 1)


def tiles_of(coefficients, step):
    first = step * TILES * WAVES
    return [coefficients[first + t * WAVES : first + (t + 1) * WAVES, :] for t in range(TILES)]


def strengths(cells, tiles, rate_rows, cap_rows, group):
    limits = pl.ds(pl.multiple_of(group * SLOTS, SLOTS), SLOTS)
    spread = jnp.sqrt(tiles[-1][:SLOTS, LANES - 1 :] / cells + EPSILON)
    return rate_rows[limits, :] * jnp.minimum(1.0, cap_rows[limits, :] / spread)


def synthesized(tiles, columns):
    high, low = split(jnp.concatenate(tiles, axis=1))
    both = dot(high, columns[...], ((0,), (0,))) + dot(low, columns[...], ((0,), (0,)))
    return both[:, :LANES] + both[:, LANES:]


def stacked(lines, strength):
    high, low = split(lines * strength)
    return jnp.concatenate([high, low, high], axis=0)


def nudge_pair(rows, stacks, models):
    pair = dot(rows[...], jnp.concatenate(stacks, axis=1), ((1,), (0,)))
    return [model + pair[:, j * LANES : (j + 1) * LANES] for j, model in enumerate(models)]


def begin_kernel(cells, own, rate_rows, cap_rows, model, rows, columns, stacks, first_nudged):
    groups = own.shape[0] // (TILES * WAVES)
    base = lax.axis_index("c") * groups
    first = []
    for step in range(groups):
        tiles = tiles_of(own, step)
        strength = strengths(cells, tiles, rate_rows, cap_rows, base + step)
        lines = synthesized(tiles, columns)
        for j in range(GROUP):
            stack = stacked(lines[j * WAVES : (j + 1) * WAVES, :], strength[j : j + 1, :])
            if step > 0:
                stacks[(step - 1) * GROUP + j] = stack
                continue
            first.append(stack)
            if j % 2:
                models = [model[base * GROUP + k] for k in (j - 1, j)]
                pair = nudge_pair(rows, first[j - 1 : j + 1], models)
                first_nudged[j - 1], first_nudged[j] = pair


def synthesis_kernel(
    cells, stacks, first_nudged, sibling, rate_rows, cap_rows, model, model_tail, rows, columns,
    nudged_hbm, nudged, along_x, strength, leaving,
):
    core = lax.axis_index("c")
    groups = model.shape[0] // GROUP
    half = groups // 2

    def ordered(step):
        return lax.rem(step + core * half, groups)

    def chunk_out(step, first, size):
        span = pl.ds(ordered(step) * GROUP + first, size)
        place = leaving.at[step * (GROUP // CHUNK) + first // CHUNK]
        here = first_nudged if step == 0 else nudged.at[step - 1]
        here = here.at[pl.ds(first, size)]
        return pltpu.make_async_copy(here, nudged_hbm.at[span], place)

    def prepare(step):
        tiles = tiles_of(sibling, step - half)
        strength[step % 2] = strengths(cells, tiles, rate_rows, cap_rows, ordered(step))
        along_x[step % 2] = synthesized(tiles, columns)

    def stack_of(step, j):
        if step < half:
            return stacks[(step - 1) * GROUP + j]
        lines = along_x[step % 2, j * WAVES : (j + 1) * WAVES, :]
        return stacked(lines, strength[step % 2, j : j + 1, :])

    def model_of(step, j):
        if step == half - 1 and j >= GROUP - TAIL:
            return model_tail[j - GROUP + TAIL]
        return model[ordered(step) * GROUP + j]

    for first in range(0, GROUP, CHUNK):
        chunk_out(0, first, CHUNK).start()
    for step in range(1, groups):
        for i in range(0, GROUP, 2):
            pair = [stack_of(step, j) for j in (i, i + 1)]
            models = [model_of(step, j) for j in (i, i + 1)]
            nudged[step - 1, i], nudged[step - 1, i + 1] = nudge_pair(rows, pair, models)
            if i == 0 and half <= step + 1 < groups:
                prepare(step + 1)
            if (i + 2) % CHUNK == 0:
                chunk_out(step, i + 2 - CHUNK, CHUNK).start()
    for step in range(groups):
        for first in range(0, GROUP, CHUNK):
            chunk_out(step, first, CHUNK).wait()


IN_HBM = pl.BlockSpec(memory_space=pltpu.HBM)
IN_VMEM = pl.BlockSpec(memory_space=pltpu.VMEM)
IN_SMEM = pl.BlockSpec(memory_space=pltpu.SMEM)


def share_kernel(chips, pieces, copies, rows):
    height = pieces.shape[0] // chips
    period = 8 * height
    total = pieces[:period, :]
    for first in range(period, pieces.shape[0], period):
        total = total + pieces[first : first + period, :]
    rows[...] = total
    for i in range(height):
        every = pl.ds(i, 8, stride=height)
        line = jnp.sum(rows[every, :], axis=0, keepdims=True)
        rows[every, :] = jnp.broadcast_to(line, (8, LANES))
    for first in range(0, pieces.shape[0], period):
        copies[first : first + period, :] = rows[...]


def share(pieces, chips):
    return pl.pallas_call(
        lambda *refs: share_kernel(chips, *refs),
        out_shape=pltpu.VMEM(pieces.shape, jnp.float32),
        in_specs=[IN_VMEM],
        out_specs=IN_VMEM,
        scratch_shapes=[pltpu.VMEM((8 * pieces.shape[0] // chips, LANES), jnp.float32)],
        compiler_params=pltpu.CompilerParams(vmem_limit_bytes=2 << 20),
        name="share",
    )(kept_in_vmem(pieces))


def kept_in_hbm(value):
    return pltpu.with_memory_space_constraint(value, pltpu.HBM)


def kept_in_vmem(value):
    return pltpu.with_memory_space_constraint(value, pltpu.VMEM)


def analysis(model, driver, rate, cap, rows, columns, rows_out, columns_out):
    groups = model.shape[0] // GROUP
    half = groups // 2
    lines = (TILES * LANES, 2 * LANES)
    sums = (8 * SLOTS, LANES)
    return pl.pallas_call(
        analysis_kernel,
        out_shape=[
            pltpu.VMEM((half * TILES * WAVES, LANES), jnp.float32),
            pltpu.VMEM((half - 1, *lines), jnp.bfloat16),
            pltpu.VMEM((half - 1, *sums), jnp.float32),
            pltpu.VMEM((GROUP - TAIL, *model.shape[1:]), jnp.float32),
            pltpu.VMEM(rows.shape[1:], jnp.bfloat16),
            pltpu.VMEM(columns.shape[1:], jnp.bfloat16),
            pltpu.VMEM(model.shape, jnp.float32),
            pltpu.VMEM((groups * SLOTS, LANES), jnp.float32),
            pltpu.VMEM((groups * SLOTS, LANES), jnp.float32),
            pltpu.VMEM(rows_out.shape[1:], jnp.bfloat16),
            pltpu.VMEM(columns_out.shape[1:], jnp.bfloat16),
        ],
        in_specs=[IN_HBM] * 8,
        out_specs=[IN_VMEM] * 11,
        scratch_shapes=[
            pltpu.VMEM((model.shape[0] - GROUP, *model.shape[1:]), jnp.float32),
            pltpu.SMEM(rate.shape, jnp.float32),
            pltpu.SMEM(cap.shape, jnp.float32),
            pltpu.VMEM((2, *lines), jnp.bfloat16),
            pltpu.VMEM((2, *sums), jnp.float32),
            pltpu.SemaphoreType.DMA((2, groups)),
            pltpu.SemaphoreType.DMA((6,)),
        ],
        compiler_params=pltpu.CompilerParams(vmem_limit_bytes=16 << 20),
        cost_estimate=estimate(2 * model.size),
        name="analysis",
    )(*map(kept_in_hbm, (model, driver, rate, cap, rows, columns, rows_out, columns_out)))


def contract(along_own, squares_own, driver_last, model, rows, columns, *fields):
    half = along_own.shape[0] + 1
    tail = (TAIL, *model.shape[1:])
    values = along_own, squares_own, driver_last, model, rows, columns
    return pl.pallas_call(
        contract_kernel,
        out_shape=[
            pltpu.VMEM((half * TILES * WAVES, LANES), jnp.float32),
            pltpu.VMEM(tail, jnp.float32),
        ],
        in_specs=[IN_VMEM] * 6 + [IN_HBM] * 2,
        out_specs=[IN_VMEM] * 2,
        scratch_shapes=[
            pltpu.VMEM(tail, jnp.float32),
            pltpu.VMEM(along_own.shape[1:], jnp.bfloat16),
            pltpu.VMEM(squares_own.shape[1:], jnp.float32),
            pltpu.SemaphoreType.DMA((2,)),
        ],
        compiler_params=pltpu.CompilerParams(vmem_limit_bytes=4 << 20),
        cost_estimate=estimate(2 * driver_last.size),
        name="contract",
    )(*map(kept_in_vmem, values), *map(kept_in_hbm, fields))


def begin(own, rate_rows, cap_rows, model, rows, columns, cells):
    fields = own.shape[0] // (TILES * WAVES) * GROUP - GROUP
    return pl.pallas_call(
        lambda *refs: begin_kernel(cells, *refs),
        out_shape=[
            pltpu.VMEM((fields, 3 * WAVES, LANES), jnp.bfloat16),
            pltpu.VMEM((GROUP, *model.shape[1:]), jnp.float32),
        ],
        in_specs=[IN_VMEM] * 6,
        out_specs=[IN_VMEM] * 2,
        compiler_params=pltpu.CompilerParams(vmem_limit_bytes=4 << 20),
        cost_estimate=estimate(fields * 3 * WAVES * LANES),
        name="begin",
    )(*map(kept_in_vmem, (own, rate_rows, cap_rows, model, rows, columns)))


def synthesis(stacks, first_nudged, sibling, limits, model, model_tail, rows, columns, cells):
    groups = model.shape[0] // GROUP
    values = stacks, first_nudged, sibling, *limits, model, model_tail, rows, columns
    return pl.pallas_call(
        lambda *refs: synthesis_kernel(cells, *refs),
        out_shape=pltpu.HBM(model.shape, jnp.float32),
        in_specs=[IN_VMEM] * 9,
        out_specs=IN_HBM,
        scratch_shapes=[
            pltpu.VMEM((groups - 1, GROUP, *model.shape[1:]), jnp.float32),
            pltpu.VMEM((2, TILES * LANES, LANES), jnp.float32),
            pltpu.VMEM((2, SLOTS, LANES), jnp.float32),
            pltpu.SemaphoreType.DMA((groups * (GROUP // CHUNK),)),
        ],
        compiler_params=pltpu.CompilerParams(vmem_limit_bytes=12 << 20),
        cost_estimate=estimate(2 * model.size),
        name="synthesis",
    )(*map(kept_in_vmem, values))


def estimate(values):
    return pl.CostEstimate(flops=600 * values, bytes_accessed=4 * values, transcendentals=0)


def per_device(model_field, driver_field, nudge_rate, increment_cap):
    fields, height, width = model_field.shape
    parts_y = lax.axis_size(("x", "c"))
    parts_x = lax.axis_size(("z", "y"))
    chips = lax.axis_size(CHIP)
    swap = [(0, 1), (1, 0)]

    high_y, low_y = split_table(height * parts_y, parts_y)
    high_x, low_x = split_table(width * parts_x, parts_x)
    turned = lambda table: np.swapaxes(table, 1, 2)
    rows_in = np.concatenate([turned(high_y), turned(low_y)], axis=1)
    columns_in = np.concatenate([turned(high_x), turned(low_x)], axis=1)
    columns_in = np.concatenate([columns_in, columns_in], axis=2)
    rows_out = np.concatenate([high_y, high_y, low_y], axis=2)
    columns_out = np.concatenate([turned(high_x), turned(low_x)], axis=2)

    other, along_own, squares_own, driver_last, rows_kept, columns_kept, *kept = analysis(
        model_field,
        driver_field,
        nudge_rate,
        increment_cap,
        rows_in,
        columns_in,
        rows_out,
        columns_out,
    )
    model_kept, rate_rows, cap_rows, rows_out_kept, columns_out_kept = kept
    arriving = lax.ppermute(other, "c", swap)
    own_lines = along_own, squares_own, driver_last
    tables_kept = rows_kept, columns_kept
    mine, model_tail = contract(
        *own_lines, model_kept, *tables_kept, model_field, driver_field
    )

    def exchanged(value):
        blocks = value.reshape(chips, 1, -1)
        return lax.all_to_all(blocks, CHIP, 0, 0, tiled=True).reshape(value.shape)

    own = exchanged(share(exchanged(mine + arriving), chips))
    sibling = lax.ppermute(own, "c", swap)
    cells = float(height * parts_y * width * parts_x)
    limits = rate_rows, cap_rows
    rest = rows_out_kept, columns_out_kept, cells
    stacks, first_nudged = begin(own, *limits, model_kept, *rest)
    return synthesis(stacks, first_nudged, sibling, limits, model_kept, model_tail, *rest)


def solution(mesh):
    finer = Mesh(mesh.devices.reshape(4, 2, 4, 4), ("x", "c", "z", "y"))
    field = P(None, ("x", "c"), ("z", "y"))
    return jax.shard_map(
        per_device,
        mesh=finer,
        in_specs=(field, field, P(), P()),
        out_specs=field,
        check_vma=False,
    )
```

```python
import numpy as np

import jax
import jax.numpy as jnp
import ml_dtypes
from jax import lax
from jax.experimental import pallas as pl
from jax.experimental.pallas import tpu as pltpu
from jax.sharding import Mesh
from jax.sharding import PartitionSpec as P

MODES = 24
WAVES = 2 * MODES
GROUP = 10
TILES = 4
LANES = 128
AHEAD = 3
CHUNK = 10
SLOTS = 16
CHIP = ("x", "z", "y")
EPSILON = 1e-06


def basis_table(length):
    positions = np.arange(length)
    wavenumber = np.concatenate([np.arange(MODES), np.arange(MODES) + 1])
    phases = positions[:, None] * wavenumber[None, :] % length
    angles = phases * (2.0 * np.pi / length)
    column = np.arange(WAVES)
    weights = np.where(column == 0, np.sqrt(1.0 / length), np.sqrt(2.0 / length))
    return np.where(column[None, :] < MODES, np.cos(angles), np.sin(angles)) * weights[None, :]


def split_table(length, parts):
    table = basis_table(length).astype(np.float32)
    high = table.astype(ml_dtypes.bfloat16)
    low = (table - high.astype(np.float32)).astype(ml_dtypes.bfloat16)
    shape = (parts, length // parts, WAVES)
    return high.reshape(shape), low.reshape(shape)


def split(value):
    high = value.astype(jnp.bfloat16)
    low = (value - high.astype(jnp.float32)).astype(jnp.bfloat16)
    return high, low


def dot(left, right, contract):
    return lax.dot_general(left, right, (contract, ((), ())), preferred_element_type=jnp.float32)


def first_contraction(difference, rows, lines, sums, i):
    folded = (difference * difference).reshape(-1, 8, LANES)
    sums[i * 8 : i * 8 + 8, :] = jnp.sum(folded, axis=0)
    product = dot(rows[...], jnp.concatenate(split(difference), axis=1), ((1,), (0,)))
    product = product[:WAVES] + product[WAVES:]
    high, low = split(product[:, :LANES] + product[:, LANES:])
    lines[i * WAVES : (i + 1) * WAVES, :LANES] = high
    lines[i * WAVES : (i + 1) * WAVES, LANES:] = low


def clear_spare(lines, sums):
    spare = (TILES * LANES - GROUP * WAVES, 2 * LANES)
    lines[GROUP * WAVES :, :] = jnp.zeros(spare, lines.dtype)
    sums[GROUP * 8 :, :] = jnp.zeros((8 * (SLOTS - GROUP), LANES), jnp.float32)


def second_contraction(columns, along_y, squares, coefficients, step):
    both = dot(columns[...], along_y[...], ((1,), (1,)))
    both = both[:WAVES] + both[WAVES:]
    total = squares[pl.ds(0, SLOTS, stride=8), :]
    for s in range(1, 8):
        total = total + squares[pl.ds(s, SLOTS, stride=8), :]
    total = jnp.sum(total, axis=1, keepdims=True)
    tiles = [both[:, t * LANES : (t + 1) * LANES] for t in range(TILES)]
    lane = lax.broadcasted_iota(jnp.int32, (SLOTS, LANES), 1)
    top = jnp.where(lane == LANES - 1, total, tiles[-1][:SLOTS])
    tiles[-1] = jnp.concatenate([top, tiles[-1][SLOTS:]], axis=0)
    first = step * TILES * WAVES
    for t in range(TILES):
        coefficients[first + t * WAVES : first + (t + 1) * WAVES, :] = tiles[t]


def analysis_kernel(
    model_hbm, driver_hbm, rate_hbm, cap_hbm, rows_hbm, columns_hbm, rows_out_hbm, columns_out_hbm,
    other, along_own, squares_own, driver_last, rows, columns, model, rate_rows, cap_rows,
    rows_out, columns_out, driver, rate, cap, along_y, squares, arrived, ready,
):
    gy, gx, core = lax.axis_index(("x", "c")), lax.axis_index(("z", "y")), lax.axis_index("c")
    groups = model.shape[0] // GROUP
    half = groups // 2
    tables = [
        pltpu.make_async_copy(rows_hbm.at[gy], rows, ready.at[0]),
        pltpu.make_async_copy(columns_hbm.at[gx], columns, ready.at[1]),
    ]
    later = [
        pltpu.make_async_copy(rate_hbm, rate, ready.at[2]),
        pltpu.make_async_copy(cap_hbm, cap, ready.at[3]),
        pltpu.make_async_copy(rows_out_hbm.at[gy], rows_out, ready.at[4]),
        pltpu.make_async_copy(columns_out_hbm.at[gx], columns_out, ready.at[5]),
    ]

    def ordered(step):
        return lax.rem(step + (1 - core) * half, groups)

    def held(step):
        if step < half:
            return along_y.at[step % 2], squares.at[step % 2]
        return along_own.at[step - half], squares_own.at[step - half]

    def fetch(step):
        span = pl.ds(ordered(step) * GROUP, GROUP)
        kept = driver_last if step == groups - 1 else driver.at[pl.ds(step * GROUP, GROUP)]
        return [
            pltpu.make_async_copy(model_hbm.at[span], model.at[span], arrived.at[0, step]),
            pltpu.make_async_copy(driver_hbm.at[span], kept, arrived.at[1, step]),
        ]

    for copy in tables + fetch(0) + later:
        copy.start()
    for step in range(1, AHEAD):
        for copy in fetch(step):
            copy.start()
    for step in [0, 1, *range(half, groups - 1)]:
        clear_spare(*held(step))

    for step in range(groups):
        for copy in (tables if step == 0 else []) + fetch(step):
            copy.wait()
        if step + AHEAD < groups:
            for copy in fetch(step + AHEAD):
                copy.start()
        for i in range(GROUP) if step < groups - 1 else []:
            difference = driver[step * GROUP + i] - model[ordered(step) * GROUP + i]
            first_contraction(difference, rows, *held(step), i)
            if i == 2 and 0 < step <= half:
                second_contraction(columns, *held(step - 1), other, step - 1)
        if step == 1:
            for copy in later:
                copy.wait()
            for field in range(model.shape[0]):
                place = field // GROUP * SLOTS + field % GROUP
                rate_rows[place : place + 1, :] = jnp.full((1, LANES), rate[field])
                cap_rows[place : place + 1, :] = jnp.full((1, LANES), cap[field])


def contract_kernel(
    along_own, squares_own, driver_last, model, rows, columns, mine, along_y, squares
):
    core = lax.axis_index("c")
    groups = model.shape[0] // GROUP
    half = groups // 2
    base = lax.rem(groups - 1 + (1 - core) * half, groups) * GROUP
    clear_spare(along_y, squares)
    for i in range(GROUP):
        first_contraction(driver_last[i] - model[base + i], rows, along_y, squares, i)
        if i % 3 == 2 and i // 3 < half - 1:
            step = i // 3
            second_contraction(columns, along_own.at[step], squares_own.at[step], mine, step)
    second_contraction(columns, along_y, squares, mine, half - 1)


def tiles_of(coefficients, step):
    first = step * TILES * WAVES
    return [coefficients[first + t * WAVES : first + (t + 1) * WAVES, :] for t in range(TILES)]


def strengths(cells, tiles, rate_rows, cap_rows, group):
    limits = pl.ds(pl.multiple_of(group * SLOTS, SLOTS), SLOTS)
    spread = jnp.sqrt(tiles[-1][:SLOTS, LANES - 1 :] / cells + EPSILON)
    return rate_rows[limits, :] * jnp.minimum(1.0, cap_rows[limits, :] / spread)


def synthesized(tiles, columns):
    high, low = split(jnp.concatenate(tiles, axis=1))
    both = dot(high, columns[...], ((0,), (0,))) + dot(low, columns[...], ((0,), (0,)))
    return both[:, :LANES] + both[:, LANES:]


def stacked(lines, strength):
    high, low = split(lines * strength)
    return jnp.concatenate([high, low, high], axis=0)


def nudge_pair(rows, stacks, models):
    pair = dot(rows[...], jnp.concatenate(stacks, axis=1), ((1,), (0,)))
    return [model + pair[:, j * LANES : (j + 1) * LANES] for j, model in enumerate(models)]


def begin_kernel(cells, own, rate_rows, cap_rows, model, rows, columns, stacks, first_nudged):
    groups = own.shape[0] // (TILES * WAVES)
    base = lax.axis_index("c") * groups
    for step in range(groups):
        tiles = tiles_of(own, step)
        strength = strengths(cells, tiles, rate_rows, cap_rows, base + step)
        lines = synthesized(tiles, columns)
        for i in range(0, GROUP, 2):
            pair = [
                stacked(lines[j * WAVES : (j + 1) * WAVES, :], strength[j : j + 1, :])
                for j in (i, i + 1)
            ]
            if step == groups - 1:
                stacks[i], stacks[i + 1] = pair
                continue
            models = [model[(base + step) * GROUP + j] for j in (i, i + 1)]
            first_nudged[step, i], first_nudged[step, i + 1] = nudge_pair(rows, pair, models)


def synthesis_kernel(
    cells, stacks, first_nudged, sibling, rate_rows, cap_rows, model, rows, columns, nudged_hbm,
    nudged, along_x, strength, leaving,
):
    core = lax.axis_index("c")
    groups = model.shape[0] // GROUP
    half = groups // 2

    def ordered(step):
        return lax.rem(step + core * half, groups)

    def chunk_out(step, first, size):
        span = pl.ds(ordered(step) * GROUP + first, size)
        place = leaving.at[step * (GROUP // CHUNK) + first // CHUNK]
        here = first_nudged.at[step] if step < half - 1 else nudged.at[step - half + 1]
        here = here.at[pl.ds(first, size)]
        return pltpu.make_async_copy(here, nudged_hbm.at[span], place)

    def prepare(step):
        tiles = tiles_of(sibling, step - half)
        strength[step % 2] = strengths(cells, tiles, rate_rows, cap_rows, ordered(step))
        along_x[step % 2] = synthesized(tiles, columns)

    def stack_of(step, j):
        if step < half:
            return stacks[j]
        lines = along_x[step % 2, j * WAVES : (j + 1) * WAVES, :]
        return stacked(lines, strength[step % 2, j : j + 1, :])

    for step in range(half - 1):
        for first in range(0, GROUP, CHUNK):
            chunk_out(step, first, CHUNK).start()
    for step in range(half - 1, groups):
        for i in range(0, GROUP, 2):
            pair = [stack_of(step, j) for j in (i, i + 1)]
            models = [model[ordered(step) * GROUP + j] for j in (i, i + 1)]
            place = step - half + 1
            nudged[place, i], nudged[place, i + 1] = nudge_pair(rows, pair, models)
            if i == 0 and half <= step + 1 < groups:
                prepare(step + 1)
            if (i + 2) % CHUNK == 0:
                chunk_out(step, i + 2 - CHUNK, CHUNK).start()
    for step in range(groups):
        for first in range(0, GROUP, CHUNK):
            chunk_out(step, first, CHUNK).wait()


IN_HBM = pl.BlockSpec(memory_space=pltpu.HBM)
IN_VMEM = pl.BlockSpec(memory_space=pltpu.VMEM)
IN_SMEM = pl.BlockSpec(memory_space=pltpu.SMEM)


def share_kernel(chips, pieces, copies, rows):
    height = pieces.shape[0] // chips
    period = 8 * height
    total = pieces[:period, :]
    for first in range(period, pieces.shape[0], period):
        total = total + pieces[first : first + period, :]
    rows[...] = total
    for i in range(height):
        every = pl.ds(i, 8, stride=height)
        line = jnp.sum(rows[every, :], axis=0, keepdims=True)
        rows[every, :] = jnp.broadcast_to(line, (8, LANES))
    for first in range(0, pieces.shape[0], period):
        copies[first : first + period, :] = rows[...]


def share(pieces, chips):
    return pl.pallas_call(
        lambda *refs: share_kernel(chips, *refs),
        out_shape=pltpu.VMEM(pieces.shape, jnp.float32),
        in_specs=[IN_VMEM],
        out_specs=IN_VMEM,
        scratch_shapes=[pltpu.VMEM((8 * pieces.shape[0] // chips, LANES), jnp.float32)],
        compiler_params=pltpu.CompilerParams(vmem_limit_bytes=2 << 20),
        name="share",
    )(kept_in_vmem(pieces))


def kept_in_hbm(value):
    return pltpu.with_memory_space_constraint(value, pltpu.HBM)


def kept_in_vmem(value):
    return pltpu.with_memory_space_constraint(value, pltpu.VMEM)


def analysis(model, driver, rate, cap, rows, columns, rows_out, columns_out):
    groups = model.shape[0] // GROUP
    half = groups // 2
    lines = (TILES * LANES, 2 * LANES)
    sums = (8 * SLOTS, LANES)
    return pl.pallas_call(
        analysis_kernel,
        out_shape=[
            pltpu.VMEM((half * TILES * WAVES, LANES), jnp.float32),
            pltpu.VMEM((half - 1, *lines), jnp.bfloat16),
            pltpu.VMEM((half - 1, *sums), jnp.float32),
            pltpu.VMEM((GROUP, *model.shape[1:]), jnp.float32),
            pltpu.VMEM(rows.shape[1:], jnp.bfloat16),
            pltpu.VMEM(columns.shape[1:], jnp.bfloat16),
            pltpu.VMEM(model.shape, jnp.float32),
            pltpu.VMEM((groups * SLOTS, LANES), jnp.float32),
            pltpu.VMEM((groups * SLOTS, LANES), jnp.float32),
            pltpu.VMEM(rows_out.shape[1:], jnp.bfloat16),
            pltpu.VMEM(columns_out.shape[1:], jnp.bfloat16),
        ],
        in_specs=[IN_HBM] * 8,
        out_specs=[IN_VMEM] * 11,
        scratch_shapes=[
            pltpu.VMEM((model.shape[0] - GROUP, *model.shape[1:]), jnp.float32),
            pltpu.SMEM(rate.shape, jnp.float32),
            pltpu.SMEM(cap.shape, jnp.float32),
            pltpu.VMEM((2, *lines), jnp.bfloat16),
            pltpu.VMEM((2, *sums), jnp.float32),
            pltpu.SemaphoreType.DMA((2, groups)),
            pltpu.SemaphoreType.DMA((6,)),
        ],
        compiler_params=pltpu.CompilerParams(vmem_limit_bytes=16 << 20),
        cost_estimate=estimate(2 * model.size),
        name="analysis",
    )(*map(kept_in_hbm, (model, driver, rate, cap, rows, columns, rows_out, columns_out)))


def contract(along_own, squares_own, driver_last, model, rows, columns):
    half = along_own.shape[0] + 1
    return pl.pallas_call(
        contract_kernel,
        out_shape=pltpu.VMEM((half * TILES * WAVES, LANES), jnp.float32),
        in_specs=[IN_VMEM] * 6,
        out_specs=IN_VMEM,
        scratch_shapes=[
            pltpu.VMEM(along_own.shape[1:], jnp.bfloat16),
            pltpu.VMEM(squares_own.shape[1:], jnp.float32),
        ],
        compiler_params=pltpu.CompilerParams(vmem_limit_bytes=4 << 20),
        cost_estimate=estimate(2 * driver_last.size),
        name="contract",
    )(*map(kept_in_vmem, (along_own, squares_own, driver_last, model, rows, columns)))


def begin(own, rate_rows, cap_rows, model, rows, columns, cells):
    groups = own.shape[0] // (TILES * WAVES)
    return pl.pallas_call(
        lambda *refs: begin_kernel(cells, *refs),
        out_shape=[
            pltpu.VMEM((GROUP, 3 * WAVES, LANES), jnp.bfloat16),
            pltpu.VMEM((groups - 1, GROUP, *model.shape[1:]), jnp.float32),
        ],
        in_specs=[IN_VMEM] * 6,
        out_specs=[IN_VMEM] * 2,
        compiler_params=pltpu.CompilerParams(vmem_limit_bytes=4 << 20),
        cost_estimate=estimate(groups * GROUP * 3 * WAVES * LANES),
        name="begin",
    )(*map(kept_in_vmem, (own, rate_rows, cap_rows, model, rows, columns)))


def synthesis(stacks, first_nudged, sibling, rate_rows, cap_rows, model, rows, columns, cells):
    groups = model.shape[0] // GROUP
    values = stacks, first_nudged, sibling, rate_rows, cap_rows, model, rows, columns
    return pl.pallas_call(
        lambda *refs: synthesis_kernel(cells, *refs),
        out_shape=pltpu.HBM(model.shape, jnp.float32),
        in_specs=[IN_VMEM] * 8,
        out_specs=IN_HBM,
        scratch_shapes=[
            pltpu.VMEM((groups // 2 + 1, GROUP, *model.shape[1:]), jnp.float32),
            pltpu.VMEM((2, TILES * LANES, LANES), jnp.float32),
            pltpu.VMEM((2, SLOTS, LANES), jnp.float32),
            pltpu.SemaphoreType.DMA((groups * (GROUP // CHUNK),)),
        ],
        compiler_params=pltpu.CompilerParams(vmem_limit_bytes=12 << 20),
        cost_estimate=estimate(2 * model.size),
        name="synthesis",
    )(*map(kept_in_vmem, values))


def estimate(values):
    return pl.CostEstimate(flops=600 * values, bytes_accessed=4 * values, transcendentals=0)


def per_device(model_field, driver_field, nudge_rate, increment_cap):
    fields, height, width = model_field.shape
    parts_y = lax.axis_size(("x", "c"))
    parts_x = lax.axis_size(("z", "y"))
    chips = lax.axis_size(CHIP)
    swap = [(0, 1), (1, 0)]

    high_y, low_y = split_table(height * parts_y, parts_y)
    high_x, low_x = split_table(width * parts_x, parts_x)
    turned = lambda table: np.swapaxes(table, 1, 2)
    rows_in = np.concatenate([turned(high_y), turned(low_y)], axis=1)
    columns_in = np.concatenate([turned(high_x), turned(low_x)], axis=1)
    columns_in = np.concatenate([columns_in, columns_in], axis=2)
    rows_out = np.concatenate([high_y, high_y, low_y], axis=2)
    columns_out = np.concatenate([turned(high_x), turned(low_x)], axis=2)

    other, along_own, squares_own, driver_last, rows_kept, columns_kept, *kept = analysis(
        model_field,
        driver_field,
        nudge_rate,
        increment_cap,
        rows_in,
        columns_in,
        rows_out,
        columns_out,
    )
    model_kept, rate_rows, cap_rows, rows_out_kept, columns_out_kept = kept
    arriving = lax.ppermute(other, "c", swap)
    mine = contract(along_own, squares_own, driver_last, model_kept, rows_kept, columns_kept)

    def exchanged(value):
        blocks = value.reshape(chips, 1, -1)
        return lax.all_to_all(blocks, CHIP, 0, 0, tiled=True).reshape(value.shape)

    own = exchanged(share(exchanged(mine + arriving), chips))
    sibling = lax.ppermute(own, "c", swap)
    cells = float(height * parts_y * width * parts_x)
    limits = rate_rows, cap_rows
    rest = model_kept, rows_out_kept, columns_out_kept, cells
    stacks, first_nudged = begin(own, *limits, *rest)
    return synthesis(stacks, first_nudged, sibling, *limits, *rest)


def solution(mesh):
    finer = Mesh(mesh.devices.reshape(4, 2, 4, 4), ("x", "c", "z", "y"))
    field = P(None, ("x", "c"), ("z", "y"))
    return jax.shard_map(
        per_device,
        mesh=finer,
        in_specs=(field, field, P(), P()),
        out_specs=field,
        check_vma=False,
    )
```

```python
import numpy as np

import jax
import jax.numpy as jnp
import ml_dtypes
from jax import lax
from jax.experimental import pallas as pl
from jax.experimental.pallas import tpu as pltpu
from jax.sharding import Mesh
from jax.sharding import PartitionSpec as P

MODES = 24
WAVES = 2 * MODES
GROUP = 10
TILES = 4
LANES = 128
AHEAD = 4
TAIL = 3
CHUNK = 10
SLOTS = 16
CHIP = ("x", "z", "y")
EPSILON = 1e-06


def basis_table(length):
    positions = np.arange(length)
    wavenumber = np.concatenate([np.arange(MODES), np.arange(MODES) + 1])
    phases = positions[:, None] * wavenumber[None, :] % length
    angles = phases * (2.0 * np.pi / length)
    column = np.arange(WAVES)
    weights = np.where(column == 0, np.sqrt(1.0 / length), np.sqrt(2.0 / length))
    return np.where(column[None, :] < MODES, np.cos(angles), np.sin(angles)) * weights[None, :]


def split_table(length, parts):
    table = basis_table(length).astype(np.float32)
    high = table.astype(ml_dtypes.bfloat16)
    low = (table - high.astype(np.float32)).astype(ml_dtypes.bfloat16)
    shape = (parts, length // parts, WAVES)
    return high.reshape(shape), low.reshape(shape)


def split(value):
    high = value.astype(jnp.bfloat16)
    low = (value - high.astype(jnp.float32)).astype(jnp.bfloat16)
    return high, low


def dot(left, right, contract):
    return lax.dot_general(left, right, (contract, ((), ())), preferred_element_type=jnp.float32)


def first_contraction(difference, rows, lines, sums, i):
    folded = (difference * difference).reshape(-1, 8, LANES)
    sums[i * 8 : i * 8 + 8, :] = jnp.sum(folded, axis=0)
    product = dot(rows[...], jnp.concatenate(split(difference), axis=1), ((1,), (0,)))
    product = product[:WAVES] + product[WAVES:]
    high, low = split(product[:, :LANES] + product[:, LANES:])
    lines[i * WAVES : (i + 1) * WAVES, :LANES] = high
    lines[i * WAVES : (i + 1) * WAVES, LANES:] = low


def clear_spare(lines, sums):
    spare = (TILES * LANES - GROUP * WAVES, 2 * LANES)
    lines[GROUP * WAVES :, :] = jnp.zeros(spare, lines.dtype)
    sums[GROUP * 8 :, :] = jnp.zeros((8 * (SLOTS - GROUP), LANES), jnp.float32)


def second_contraction(columns, along_y, squares, coefficients, step):
    both = dot(columns[...], along_y[...], ((1,), (1,)))
    both = both[:WAVES] + both[WAVES:]
    total = squares[pl.ds(0, SLOTS, stride=8), :]
    for s in range(1, 8):
        total = total + squares[pl.ds(s, SLOTS, stride=8), :]
    total = jnp.sum(total, axis=1, keepdims=True)
    tiles = [both[:, t * LANES : (t + 1) * LANES] for t in range(TILES)]
    lane = lax.broadcasted_iota(jnp.int32, (SLOTS, LANES), 1)
    top = jnp.where(lane == LANES - 1, total, tiles[-1][:SLOTS])
    tiles[-1] = jnp.concatenate([top, tiles[-1][SLOTS:]], axis=0)
    first = step * TILES * WAVES
    for t in range(TILES):
        coefficients[first + t * WAVES : first + (t + 1) * WAVES, :] = tiles[t]


def analysis_kernel(
    model_hbm, driver_hbm, rate_hbm, cap_hbm, rows_hbm, columns_hbm, rows_out_hbm, columns_out_hbm,
    other, along_own, squares_own, driver_last, rows, columns, model, rate_rows, cap_rows,
    rows_out, columns_out, driver, rate, cap, along_y, squares, arrived, ready,
):
    gy, gx, core = lax.axis_index(("x", "c")), lax.axis_index(("z", "y")), lax.axis_index("c")
    groups = model.shape[0] // GROUP
    half = groups // 2
    tables = [
        pltpu.make_async_copy(rows_hbm.at[gy], rows, ready.at[0]),
        pltpu.make_async_copy(columns_hbm.at[gx], columns, ready.at[1]),
    ]
    later = [
        pltpu.make_async_copy(rate_hbm, rate, ready.at[2]),
        pltpu.make_async_copy(cap_hbm, cap, ready.at[3]),
        pltpu.make_async_copy(rows_out_hbm.at[gy], rows_out, ready.at[4]),
        pltpu.make_async_copy(columns_out_hbm.at[gx], columns_out, ready.at[5]),
    ]

    def ordered(step):
        return lax.rem(step + (1 - core) * half, groups)

    def held(step):
        if step < half:
            return along_y.at[step % 2], squares.at[step % 2]
        return along_own.at[step - half], squares_own.at[step - half]

    def fetch(step):
        last = step == groups - 1
        span = pl.ds(ordered(step) * GROUP, GROUP - TAIL if last else GROUP)
        kept = driver_last if last else driver.at[pl.ds(step * GROUP, GROUP)]
        return [
            pltpu.make_async_copy(model_hbm.at[span], model.at[span], arrived.at[0, step]),
            pltpu.make_async_copy(driver_hbm.at[span], kept, arrived.at[1, step]),
        ]

    for copy in tables + fetch(0) + later:
        copy.start()
    for step in range(1, AHEAD):
        for copy in fetch(step):
            copy.start()
    for step in [0, 1, *range(half, groups - 1)]:
        clear_spare(*held(step))

    for step in range(groups):
        for copy in (tables if step == 0 else []) + fetch(step):
            copy.wait()
        if step + AHEAD < groups:
            for copy in fetch(step + AHEAD):
                copy.start()
        for i in range(GROUP) if step < groups - 1 else []:
            difference = driver[step * GROUP + i] - model[ordered(step) * GROUP + i]
            first_contraction(difference, rows, *held(step), i)
            if i == 2 and 0 < step <= half:
                second_contraction(columns, *held(step - 1), other, step - 1)
        if step == 1:
            for copy in later:
                copy.wait()
            for field in range(model.shape[0]):
                place = field // GROUP * SLOTS + field % GROUP
                rate_rows[place : place + 1, :] = jnp.full((1, LANES), rate[field])
                cap_rows[place : place + 1, :] = jnp.full((1, LANES), cap[field])


def contract_kernel(
    along_own, squares_own, driver_last, model, rows, columns, model_hbm, driver_hbm,
    mine, model_tail, driver_tail, along_y, squares, arrived,
):
    core = lax.axis_index("c")
    groups = model.shape[0] // GROUP
    half = groups // 2
    base = lax.rem(groups - 1 + (1 - core) * half, groups) * GROUP
    span = pl.ds(base + GROUP - TAIL, TAIL)
    copies = [
        pltpu.make_async_copy(model_hbm.at[span], model_tail, arrived.at[0]),
        pltpu.make_async_copy(driver_hbm.at[span], driver_tail, arrived.at[1]),
    ]
    for copy in copies:
        copy.start()
    clear_spare(along_y, squares)
    for i in range(GROUP - TAIL):
        first_contraction(driver_last[i] - model[base + i], rows, along_y, squares, i)
        if i % 2 and i // 2 < half - 1:
            step = i // 2
            second_contraction(columns, along_own.at[step], squares_own.at[step], mine, step)
    for copy in copies:
        copy.wait()
    for i in range(TAIL):
        difference = driver_tail[i] - model_tail[i]
        first_contraction(difference, rows, along_y, squares, GROUP - TAIL + i)
    second_contraction(columns, along_y, squares, mine, half - 1)


def tiles_of(coefficients, step):
    first = step * TILES * WAVES
    return [coefficients[first + t * WAVES : first + (t + 1) * WAVES, :] for t in range(TILES)]


def strengths(cells, tiles, rate_rows, cap_rows, group):
    limits = pl.ds(pl.multiple_of(group * SLOTS, SLOTS), SLOTS)
    spread = jnp.sqrt(tiles[-1][:SLOTS, LANES - 1 :] / cells + EPSILON)
    return rate_rows[limits, :] * jnp.minimum(1.0, cap_rows[limits, :] / spread)


def synthesized(tiles, columns):
    high, low = split(jnp.concatenate(tiles, axis=1))
    both = dot(high, columns[...], ((0,), (0,))) + dot(low, columns[...], ((0,), (0,)))
    return both[:, :LANES] + both[:, LANES:]


def stacked(lines, strength):
    high, low = split(lines * strength)
    return jnp.concatenate([high, low, high], axis=0)


def nudge_pair(rows, stacks, models):
    pair = dot(rows[...], jnp.concatenate(stacks, axis=1), ((1,), (0,)))
    return [model + pair[:, j * LANES : (j + 1) * LANES] for j, model in enumerate(models)]


def begin_kernel(cells, own, rate_rows, cap_rows, model, rows, columns, stacks, first_nudged):
    groups = own.shape[0] // (TILES * WAVES)
    base = lax.axis_index("c") * groups
    first = []
    for step in range(groups):
        tiles = tiles_of(own, step)
        strength = strengths(cells, tiles, rate_rows, cap_rows, base + step)
        lines = synthesized(tiles, columns)
        for j in range(GROUP):
            stack = stacked(lines[j * WAVES : (j + 1) * WAVES, :], strength[j : j + 1, :])
            if step > 0:
                stacks[(step - 1) * GROUP + j] = stack
                continue
            first.append(stack)
            if j % 2:
                models = [model[base * GROUP + k] for k in (j - 1, j)]
                pair = nudge_pair(rows, first[j - 1 : j + 1], models)
                first_nudged[j - 1], first_nudged[j] = pair


def synthesis_kernel(
    cells, stacks, first_nudged, sibling, rate_rows, cap_rows, model, model_tail, rows, columns,
    nudged_hbm, nudged, along_x, strength, leaving,
):
    core = lax.axis_index("c")
    groups = model.shape[0] // GROUP
    half = groups // 2

    def ordered(step):
        return lax.rem(step + core * half, groups)

    def chunk_out(step, first, size):
        span = pl.ds(ordered(step) * GROUP + first, size)
        place = leaving.at[step * (GROUP // CHUNK) + first // CHUNK]
        here = first_nudged if step == 0 else nudged.at[step - 1]
        here = here.at[pl.ds(first, size)]
        return pltpu.make_async_copy(here, nudged_hbm.at[span], place)

    def prepare(step):
        tiles = tiles_of(sibling, step - half)
        strength[step % 2] = strengths(cells, tiles, rate_rows, cap_rows, ordered(step))
        along_x[step % 2] = synthesized(tiles, columns)

    def stack_of(step, j):
        if step < half:
            return stacks[(step - 1) * GROUP + j]
        lines = along_x[step % 2, j * WAVES : (j + 1) * WAVES, :]
        return stacked(lines, strength[step % 2, j : j + 1, :])

    def model_of(step, j):
        if step == half - 1 and j >= GROUP - TAIL:
            return model_tail[j - GROUP + TAIL]
        return model[ordered(step) * GROUP + j]

    for first in range(0, GROUP, CHUNK):
        chunk_out(0, first, CHUNK).start()
    for step in range(1, groups):
        for i in range(0, GROUP, 2):
            pair = [stack_of(step, j) for j in (i, i + 1)]
            models = [model_of(step, j) for j in (i, i + 1)]
            nudged[step - 1, i], nudged[step - 1, i + 1] = nudge_pair(rows, pair, models)
            if i == 0 and half <= step + 1 < groups:
                prepare(step + 1)
            if (i + 2) % CHUNK == 0:
                chunk_out(step, i + 2 - CHUNK, CHUNK).start()
    for step in range(groups):
        for first in range(0, GROUP, CHUNK):
            chunk_out(step, first, CHUNK).wait()


IN_HBM = pl.BlockSpec(memory_space=pltpu.HBM)
IN_VMEM = pl.BlockSpec(memory_space=pltpu.VMEM)
IN_SMEM = pl.BlockSpec(memory_space=pltpu.SMEM)


def share_kernel(chips, pieces, copies, rows):
    height = pieces.shape[0] // chips
    period = 8 * height
    total = pieces[:period, :]
    for first in range(period, pieces.shape[0], period):
        total = total + pieces[first : first + period, :]
    rows[...] = total
    for i in range(height):
        every = pl.ds(i, 8, stride=height)
        line = jnp.sum(rows[every, :], axis=0, keepdims=True)
        rows[every, :] = jnp.broadcast_to(line, (8, LANES))
    for first in range(0, pieces.shape[0], period):
        copies[first : first + period, :] = rows[...]


def share(pieces, chips):
    return pl.pallas_call(
        lambda *refs: share_kernel(chips, *refs),
        out_shape=pltpu.VMEM(pieces.shape, jnp.float32),
        in_specs=[IN_VMEM],
        out_specs=IN_VMEM,
        scratch_shapes=[pltpu.VMEM((8 * pieces.shape[0] // chips, LANES), jnp.float32)],
        compiler_params=pltpu.CompilerParams(vmem_limit_bytes=2 << 20),
        name="share",
    )(kept_in_vmem(pieces))


def kept_in_hbm(value):
    return pltpu.with_memory_space_constraint(value, pltpu.HBM)


def kept_in_vmem(value):
    return pltpu.with_memory_space_constraint(value, pltpu.VMEM)


def analysis(model, driver, rate, cap, rows, columns, rows_out, columns_out):
    groups = model.shape[0] // GROUP
    half = groups // 2
    lines = (TILES * LANES, 2 * LANES)
    sums = (8 * SLOTS, LANES)
    return pl.pallas_call(
        analysis_kernel,
        out_shape=[
            pltpu.VMEM((half * TILES * WAVES, LANES), jnp.float32),
            pltpu.VMEM((half - 1, *lines), jnp.bfloat16),
            pltpu.VMEM((half - 1, *sums), jnp.float32),
            pltpu.VMEM((GROUP - TAIL, *model.shape[1:]), jnp.float32),
            pltpu.VMEM(rows.shape[1:], jnp.bfloat16),
            pltpu.VMEM(columns.shape[1:], jnp.bfloat16),
            pltpu.VMEM(model.shape, jnp.float32),
            pltpu.VMEM((groups * SLOTS, LANES), jnp.float32),
            pltpu.VMEM((groups * SLOTS, LANES), jnp.float32),
            pltpu.VMEM(rows_out.shape[1:], jnp.bfloat16),
            pltpu.VMEM(columns_out.shape[1:], jnp.bfloat16),
        ],
        in_specs=[IN_HBM] * 8,
        out_specs=[IN_VMEM] * 11,
        scratch_shapes=[
            pltpu.VMEM((model.shape[0] - GROUP, *model.shape[1:]), jnp.float32),
            pltpu.SMEM(rate.shape, jnp.float32),
            pltpu.SMEM(cap.shape, jnp.float32),
            pltpu.VMEM((2, *lines), jnp.bfloat16),
            pltpu.VMEM((2, *sums), jnp.float32),
            pltpu.SemaphoreType.DMA((2, groups)),
            pltpu.SemaphoreType.DMA((6,)),
        ],
        compiler_params=pltpu.CompilerParams(vmem_limit_bytes=16 << 20),
        cost_estimate=estimate(2 * model.size),
        name="analysis",
    )(*map(kept_in_hbm, (model, driver, rate, cap, rows, columns, rows_out, columns_out)))


def contract(along_own, squares_own, driver_last, model, rows, columns, *fields):
    half = along_own.shape[0] + 1
    tail = (TAIL, *model.shape[1:])
    values = along_own, squares_own, driver_last, model, rows, columns
    return pl.pallas_call(
        contract_kernel,
        out_shape=[
            pltpu.VMEM((half * TILES * WAVES, LANES), jnp.float32),
            pltpu.VMEM(tail, jnp.float32),
        ],
        in_specs=[IN_VMEM] * 6 + [IN_HBM] * 2,
        out_specs=[IN_VMEM] * 2,
        scratch_shapes=[
            pltpu.VMEM(tail, jnp.float32),
            pltpu.VMEM(along_own.shape[1:], jnp.bfloat16),
            pltpu.VMEM(squares_own.shape[1:], jnp.float32),
            pltpu.SemaphoreType.DMA((2,)),
        ],
        compiler_params=pltpu.CompilerParams(vmem_limit_bytes=4 << 20),
        cost_estimate=estimate(2 * driver_last.size),
        name="contract",
    )(*map(kept_in_vmem, values), *map(kept_in_hbm, fields))


def begin(own, rate_rows, cap_rows, model, rows, columns, cells):
    fields = own.shape[0] // (TILES * WAVES) * GROUP - GROUP
    return pl.pallas_call(
        lambda *refs: begin_kernel(cells, *refs),
        out_shape=[
            pltpu.VMEM((fields, 3 * WAVES, LANES), jnp.bfloat16),
            pltpu.VMEM((GROUP, *model.shape[1:]), jnp.float32),
        ],
        in_specs=[IN_VMEM] * 6,
        out_specs=[IN_VMEM] * 2,
        compiler_params=pltpu.CompilerParams(vmem_limit_bytes=4 << 20),
        cost_estimate=estimate(fields * 3 * WAVES * LANES),
        name="begin",
    )(*map(kept_in_vmem, (own, rate_rows, cap_rows, model, rows, columns)))


def synthesis(stacks, first_nudged, sibling, limits, model, model_tail, rows, columns, cells):
    groups = model.shape[0] // GROUP
    values = stacks, first_nudged, sibling, *limits, model, model_tail, rows, columns
    return pl.pallas_call(
        lambda *refs: synthesis_kernel(cells, *refs),
        out_shape=pltpu.HBM(model.shape, jnp.float32),
        in_specs=[IN_VMEM] * 9,
        out_specs=IN_HBM,
        scratch_shapes=[
            pltpu.VMEM((groups - 1, GROUP, *model.shape[1:]), jnp.float32),
            pltpu.VMEM((2, TILES * LANES, LANES), jnp.float32),
            pltpu.VMEM((2, SLOTS, LANES), jnp.float32),
            pltpu.SemaphoreType.DMA((groups * (GROUP // CHUNK),)),
        ],
        compiler_params=pltpu.CompilerParams(vmem_limit_bytes=12 << 20),
        cost_estimate=estimate(2 * model.size),
        name="synthesis",
    )(*map(kept_in_vmem, values))


def estimate(values):
    return pl.CostEstimate(flops=600 * values, bytes_accessed=4 * values, transcendentals=0)


def per_device(model_field, driver_field, nudge_rate, increment_cap):
    fields, height, width = model_field.shape
    parts_y = lax.axis_size(("x", "c"))
    parts_x = lax.axis_size(("z", "y"))
    chips = lax.axis_size(CHIP)
    swap = [(0, 1), (1, 0)]

    high_y, low_y = split_table(height * parts_y, parts_y)
    high_x, low_x = split_table(width * parts_x, parts_x)
    turned = lambda table: np.swapaxes(table, 1, 2)
    rows_in = np.concatenate([turned(high_y), turned(low_y)], axis=1)
    columns_in = np.concatenate([turned(high_x), turned(low_x)], axis=1)
    columns_in = np.concatenate([columns_in, columns_in], axis=2)
    rows_out = np.concatenate([high_y, high_y, low_y], axis=2)
    columns_out = np.concatenate([turned(high_x), turned(low_x)], axis=2)

    other, along_own, squares_own, driver_last, rows_kept, columns_kept, *kept = analysis(
        model_field,
        driver_field,
        nudge_rate,
        increment_cap,
        rows_in,
        columns_in,
        rows_out,
        columns_out,
    )
    model_kept, rate_rows, cap_rows, rows_out_kept, columns_out_kept = kept
    arriving = lax.ppermute(other, "c", swap)
    own_lines = along_own, squares_own, driver_last
    tables_kept = rows_kept, columns_kept
    mine, model_tail = contract(
        *own_lines, model_kept, *tables_kept, model_field, driver_field
    )

    def exchanged(value):
        blocks = value.reshape(chips, 1, -1)
        return lax.all_to_all(blocks, CHIP, 0, 0, tiled=True).reshape(value.shape)

    own = exchanged(share(exchanged(mine + arriving), chips))
    sibling = lax.ppermute(own, "c", swap)
    cells = float(height * parts_y * width * parts_x)
    limits = rate_rows, cap_rows
    rest = rows_out_kept, columns_out_kept, cells
    stacks, first_nudged = begin(own, *limits, model_kept, *rest)
    return synthesis(stacks, first_nudged, sibling, limits, model_kept, model_tail, *rest)


def solution(mesh):
    finer = Mesh(mesh.devices.reshape(4, 2, 4, 4), ("x", "c", "z", "y"))
    field = P(None, ("x", "c"), ("z", "y"))
    return jax.shard_map(
        per_device,
        mesh=finer,
        in_specs=(field, field, P(), P()),
        out_specs=field,
        check_vma=False,
    )
```
